256 devices in a mesh: lon: 16 (over y_hi, z), lat: 4 (over x), grp: 4 (over y_lo, core).
Axes of the slice: x: 4, y: 4 (y_hi: 2, y_lo: 2; y = y_hi * 2 + y_lo), z: 8, core: 2. Of those that a mesh axis runs over, the one named last changes fastest.
Arguments:
- sea_surface: float32 [16, 256, 8192], P('grp', 'lat', 'lon'), may hold values from -6 to 6
- velocity: float32 [2, 16, 256, 8192], P(None, 'grp', 'lat', 'lon'), may hold values from -2 to 2
- levels: int32 [256, 8192], P('lat', 'lon'), may hold values from 1 to 50
- wind_basis: bfloat16 [16, 256, 8192], P(None, 'lat', 'lon'), may hold values from -1.5 to 1.5
- proposals: float32 [16, 16], replicated, may hold values from -4 to 4
- member_ids: int32 [16], replicated, may hold values from 0 to 15, each once
- conv_weight: bfloat16 [128, 256], replicated, may hold values from -0.5 to 0.5
- couple_in: float32 [264, 512], replicated, may hold values from -0.375 to 0.375
- couple_in_bias: float32 [512], replicated, may hold values from -3 to 3
- couple_out: float32 [512, 16], replicated, may hold values from -0.25 to 0.25
- couple_out_bias: float32 [16], replicated, may hold values from -3 to 3
Outputs:
- surface_out: float32 [16, 256, 8192], P('grp', 'lat', 'lon')
- velocity_out: float32 [2, 16, 256, 8192], P(None, 'grp', 'lat', 'lon')
- summary: float32 [16, 4, 4, 2, 256], P('lon', 'lat', 'grp')
- weight_step: float32 [176656], replicated
The draws below stay inside these ranges and needn't reach their ends.
Inputs may be any that keep to these rules, and one draw needn't show every extreme that they name: member_ids is a permutation of 0 to 15.
All inputs are finite; a program needn't handle non-finite values.
Results may differ from the reference program's by a relative error of at most 0.0031.
Values may be sent and summed in bfloat16 or wider, within the bound.
A program may use at most 128 MiB of HBM per device.

```python
import math
from functools import partial
import jax
import jax.numpy as jnp
from jax import lax

CY = 64
MEM_DEV = 4
STEPS = 8
NLEV = 50
PH = 8
PW = 16
FEAT = 256
HID = 512
PDIM = 16
HALF = 8
MEMBERS = 16
NY = 256
NX = 8192
ITEMS_DEV = 2
N_LON = 16
N_LAT = 4
N_GRP = 4


def set_ends(entries, stream_key, least, top_value):
    extent = entries.shape
    index_at = [jax.random.randint(jax.random.fold_in(stream_key, axis), (), 0, extent[axis]) for axis in range(len(extent))]
    entries = entries.at[tuple(index_at)].set(least)
    longest = extent.index(max(extent))
    index_at[longest] = (index_at[longest] + 1) % extent[longest]
    return entries.at[tuple(index_at)].set(top_value)


def steps_of(stream_key, dims, pieces, low, high):
    gain, own = 1.0, jax.random.fold_in(stream_key, 6)
    for dim, blocks in pieces:
        steps = jnp.exp(jax.random.uniform(jax.random.fold_in(own, dim), (blocks,), jnp.float32, low / len(pieces), high / len(pieces)))
        gain = gain * jnp.repeat(steps, dims[dim] // blocks).reshape([-1 if axis == dim else 1 for axis in range(len(dims))])
    return gain


def scatter_about(own_key, shape, spread, most, cuts=(), held_as=jnp.bfloat16):
    loudness = steps_of(own_key, shape, cuts, -0.22, 0.18) if cuts else 1.0
    entries = jax.random.normal(own_key, shape, jnp.float32) * spread * loudness
    return jnp.minimum(jnp.maximum(entries, -most), most).astype(held_as)


def setup_inputs(seed: int = 0) -> dict:
    arg_keys = jax.random.split(jax.random.key(seed), 12)
    return {
        "sea_surface": scatter_about(arg_keys[0], (MEMBERS, NY, NX), 1.0, 6.0, ((0, 4), (1, 4), (2, 16)), jnp.float32),
        "velocity": scatter_about(arg_keys[1], (2, MEMBERS, NY, NX), 0.3, 2.0, ((1, 4), (2, 4), (3, 16)), jnp.float32),
        "levels": set_ends(jax.random.randint(arg_keys[2], (NY, NX), 1, NLEV + 1), jax.random.fold_in(arg_keys[2], 1), 1, NLEV).astype(jnp.int32),
        "wind_basis": scatter_about(arg_keys[3], (PDIM, NY, NX), PDIM ** -0.5, 1.5, ((1, 4), (2, 16))),
        "proposals": scatter_about(arg_keys[4], (MEMBERS, PDIM), 1.0, 4.0, (), jnp.float32),
        "member_ids": jax.random.permutation(arg_keys[5], MEMBERS).astype(jnp.int32),
        "conv_weight": scatter_about(arg_keys[6], (PH * PW, FEAT), (PH * PW) ** -0.5, 0.5),
        "couple_in": scatter_about(arg_keys[7], (HALF + FEAT, HID), (HALF + FEAT) ** -0.5, 0.375, (), jnp.float32),
        "couple_in_bias": scatter_about(arg_keys[8], (HID,), 0.5, 3.0, (), jnp.float32),
        "couple_out": scatter_about(arg_keys[9], (HID, PDIM), HID ** -0.5, 0.25, (), jnp.float32),
        "couple_out_bias": scatter_about(arg_keys[10], (PDIM,), 0.5, 3.0, (), jnp.float32),
    }


GRAVITY = 0.45
DRAG_RATE = 0.02
CORI_BASE = 0.05
CORI_SLOPE = 0.1
WIND_SCALE = 0.05
EPSILON = 1e-06
PRECISE = lax.Precision.HIGHEST

def advance(sea_level, east_flow, north_flow, hu_face, hv_face, forcing, cori_u, cori_v):
    flux_x = hu_face * east_flow
    flux_y = hv_face * north_flow
    zero_row = jnp.zeros_like(flux_y[:1])
    flux_y_up = jnp.concatenate([flux_y[1:], zero_row], axis=0)
    new_level = sea_level - (jnp.roll(flux_x, -1, axis=1) - flux_x + flux_y_up - flux_y)
    north_up = jnp.concatenate([north_flow[1:], zero_row], axis=0)
    east_down = jnp.concatenate([zero_row, east_flow[:-1]], axis=0)
    v_mean = 0.25 * (north_flow + north_up + jnp.roll(north_flow, 1, axis=1) + jnp.roll(north_up, 1, axis=1))
    u_mean = 0.25 * (east_flow + jnp.roll(east_flow, -1, axis=1) + east_down + jnp.roll(east_down, -1, axis=1))
    level_down = jnp.concatenate([zero_row, new_level[:-1]], axis=0)
    new_east = east_flow + cori_u * v_mean - GRAVITY * (new_level - jnp.roll(new_level, 1, axis=1)) - DRAG_RATE * east_flow + forcing
    new_north = north_flow - cori_v * u_mean - GRAVITY * (new_level - level_down) - DRAG_RATE * north_flow
    return (new_level, new_east, new_north)

def to_patches(band_rows, kernel_rows, kernel_cols):
    count, height, breadth = band_rows.shape
    blocks = band_rows.reshape(count, height // kernel_rows, kernel_rows, breadth // kernel_cols, kernel_cols)
    return blocks.transpose(0, 1, 3, 2, 4).reshape(-1, kernel_rows * kernel_cols)

def flow_loss(params, w_in, b_in, w_out, b_out, summary):
    half_count = params.shape[1] // 2
    lower = params[:, :half_count]
    upper = params[:, half_count:]
    context = jnp.concatenate([lower, summary], axis=1)
    hidden = jnp.tanh(jnp.dot(context, w_in, precision=PRECISE) + b_in)
    out_raw = jnp.dot(hidden, w_out, precision=PRECISE) + b_out
    log_scale = jnp.tanh(out_raw[:, :half_count])
    latent = upper * jnp.exp(log_scale) + out_raw[:, half_count:]
    return jnp.sum(0.5 * latent * latent - log_scale)

def reference(sea_surface, velocity, levels, wind_basis, proposals, member_ids, conv_weight, couple_in, couple_in_bias, couple_out, couple_out_bias):
    sea_depth = levels.astype(jnp.float32) / NLEV
    hu_face = 0.5 * (sea_depth + jnp.roll(sea_depth, 1, axis=1))
    hv_face = 0.5 * (sea_depth + jnp.concatenate([jnp.zeros_like(sea_depth[:1]), sea_depth[:-1]], axis=0))
    row_index = jnp.arange(NY).astype(jnp.float32)[:, None]
    cori_u = CORI_BASE + CORI_SLOPE * (row_index + 0.5) / NY
    cori_v = CORI_BASE + CORI_SLOPE * row_index / NY
    coeff_rows = proposals[member_ids].astype(jnp.bfloat16)
    basis_flat = wind_basis.reshape(PDIM, NY * NX)

    def evolve(inputs):
        sea_level, east_flow, north_flow, coeffs = inputs
        forcing = WIND_SCALE * jnp.dot(coeffs[None, :], basis_flat, preferred_element_type=jnp.float32).reshape(NY, NX)
        frames = []
        for step_index in range(STEPS):
            sea_level, east_flow, north_flow = advance(sea_level, east_flow, north_flow, hu_face, hv_face, forcing, cori_u, cori_v)
            frames.append(sea_level.astype(jnp.bfloat16))
        return (sea_level, east_flow, north_flow, jnp.stack(frames))
    surface_out, east_out, north_out, frames = lax.map(evolve, (sea_surface, velocity[0], velocity[1], coeff_rows))
    velocity_out = jnp.stack([east_out, north_out])
    band_rows = frames.reshape(N_GRP, MEM_DEV, STEPS, N_LAT, CY, NX).transpose(3, 0, 2, 1, 4, 5)
    band_rows = band_rows.reshape(N_LAT, N_GRP, N_LON, ITEMS_DEV, CY, NX).transpose(2, 0, 1, 3, 4, 5).reshape(-1, CY, NX)
    lon_ids = jnp.arange(N_LON, dtype=jnp.int32)[:, None, None, None]
    grp_ids = jnp.arange(N_GRP, dtype=jnp.int32)[None, None, :, None]
    item_ids = jnp.arange(ITEMS_DEV, dtype=jnp.int32)[None, None, None, :]
    members = grp_ids * MEM_DEV + (lon_ids * ITEMS_DEV + item_ids) % MEM_DEV
    members = jnp.broadcast_to(members, (N_LON, N_LAT, N_GRP, ITEMS_DEV)).reshape(-1)
    params = proposals[member_ids[members]]
    inv_root = 1.0 / math.sqrt(CY // PH * (NX // PW))

    def embed_band(band):
        patch_rows = to_patches(band[None], PH, PW)
        activation = jnp.tanh(jnp.dot(patch_rows, conv_weight, preferred_element_type=jnp.float32))
        return lax.optimization_barrier(jnp.sum(activation, axis=0)) * inv_root
    summary = lax.map(embed_band, band_rows)
    loss_value, pullback = jax.vjp(partial(flow_loss, params), couple_in, couple_in_bias, couple_out, couple_out_bias, summary)
    g_in, g_in_b, g_out, g_out_b, d_summary = pullback(jnp.ones_like(loss_value))

    def conv_grad(running, inputs):
        band, d_item = inputs
        patch_rows = to_patches(band[None], PH, PW)
        activation = jnp.tanh(jnp.dot(patch_rows, conv_weight, preferred_element_type=jnp.float32))
        d_pre = ((d_item * inv_root)[None, :] * (1.0 - activation * activation)).astype(jnp.bfloat16)
        return (running + lax.dot_general(patch_rows, d_pre, (((0,), (0,)), ((), ())), preferred_element_type=jnp.float32), None)
    g_conv, unused = lax.scan(conv_grad, jnp.zeros((PH * PW, FEAT), jnp.float32), (band_rows, d_summary))
    grad_total = jnp.concatenate([g_conv.reshape(-1), g_in.reshape(-1), g_in_b, g_out.reshape(-1), g_out_b])
    weight_step = -grad_total / jnp.sqrt(jnp.mean(grad_total * grad_total) + EPSILON)
    return (surface_out, velocity_out, summary.reshape(N_LON, N_LAT, N_GRP, ITEMS_DEV, FEAT), weight_step)
```

```python
import functools
import math

import jax
import jax.numpy as jnp
from jax import lax
from jax.experimental import pallas as pl
from jax.experimental.pallas import tpu as pltpu
from jax.sharding import PartitionSpec as P

STEPS = 8
NLEV = 50
PH = 8
PW = 16
GRAVITY = 0.45
DRAG_RATE = 0.02
CORI_BASE = 0.05
CORI_SLOPE = 0.1
WIND_SCALE = 0.05
EPSILON = 1e-06
HALF = 8
LANES = 128
F32 = jnp.float32
BF16 = jnp.bfloat16
PRECISE = lax.Precision.HIGHEST
MESH = pl.DeviceIdType.MESH
VMEM = pl.BlockSpec(memory_space=pltpu.VMEM)
SMEM = pl.BlockSpec(memory_space=pltpu.SMEM)


def iota(shape, dim):
    return lax.broadcasted_iota(jnp.int32, shape, dim)


def halo_kernel(
    ids_ref, prop_ref, sea_ref, vel_ref, lev_ref, wind_ref,
    frc_ref, rowf_ref, rowl_ref, colf_ref, coll_ref, corf_ref, corl_ref,
    east_ref, west_ref, send_sem, recv_sem,
):
    members, rows, cols = sea_ref.shape
    n_lon, n_lat = lax.axis_size("lon"), lax.axis_size("lat")
    lon, lat, grp = lax.axis_index("lon"), lax.axis_index("lat"), lax.axis_index("grp")
    east, west = lax.rem(lon + 1, n_lon), lax.rem(lon + n_lon - 1, n_lon)
    north, south = lax.rem(lat + 1, n_lat), lax.rem(lat + n_lat - 1, n_lat)

    barrier = pltpu.get_barrier_semaphore()
    for to_lat in (lat, north, south):
        for to_lon in (lon, east, west):
            if to_lat is lat and to_lon is lon:
                continue
            pl.semaphore_signal(
                barrier, inc=1, device_id={"lon": to_lon, "lat": to_lat}, device_id_type=MESH
            )

    coeffs = []
    for m in range(members):
        row = ids_ref[grp * members + m]
        for k in range(wind_ref.shape[0]):
            full = prop_ref[row, k]
            scaled = full * 65537.0
            coeffs.append(scaled - (scaled - full))

    def force(r, carry):
        at = pl.ds(pl.multiple_of(r * 16, 16), 16)
        total = [None] * members
        for k in range(wind_ref.shape[0]):
            wind = wind_ref[k, at, :].astype(F32)
            for m in range(members):
                term = coeffs[m * wind_ref.shape[0] + k] * wind
                total[m] = term if k == 0 else total[m] + term
        for m in range(members):
            frc_ref[m, at, :] = WIND_SCALE * total[m]
        return carry

    lax.fori_loop(0, rows // 16, force, 0)

    slot = iota((rows, LANES), 1) // 8
    fields = [(sea_ref, m) for m in range(members)]
    fields += [(vel_ref, m) for m in range(2 * members)]
    fields += [(frc_ref, m) for m in range(members)]
    pack_east = jnp.zeros((rows, LANES), F32)
    pack_west = jnp.zeros((rows, LANES), F32)
    for s, (ref, m) in enumerate(fields):
        right = ref[m, :, cols - LANES :]
        left = ref[m, :, :LANES]
        pack_east = jnp.where(slot == s, pltpu.roll(right, (8 * s + 8) % LANES, 1), pack_east)
        pack_west = jnp.where(slot == s, pltpu.roll(left, 8 * s, 1) if s else left, pack_west)
    east_ref[...] = pack_east
    west_ref[...] = pack_west

    pl.semaphore_wait(barrier, 8)

    copies = []

    def send(src, dst, to_lat, to_lon):
        i = len(copies)
        copy = pltpu.make_async_remote_copy(
            src_ref=src, dst_ref=dst, send_sem=send_sem.at[i], recv_sem=recv_sem.at[i],
            device_id={"lon": to_lon, "lat": to_lat}, device_id_type=MESH,
        )
        copy.start()
        copies.append(copy)

    for side, to_lat, first, wide in ((0, north, rows - 8, rows - 16), (1, south, 0, 0)):
        send(sea_ref.at[:, first : first + 8], rowf_ref.at[side, 0:members], to_lat, lon)
        send(vel_ref.at[:, first : first + 8], rowf_ref.at[side, members : 3 * members], to_lat, lon)
        send(frc_ref.at[:, first : first + 8], rowf_ref.at[side, 3 * members :], to_lat, lon)
        send(lev_ref.at[wide : wide + 16], rowl_ref.at[side], to_lat, lon)
    for side, to_lon, ref, first in ((0, east, east_ref, cols - LANES), (1, west, west_ref, 0)):
        send(ref, colf_ref.at[side], lat, to_lon)
        send(lev_ref.at[:, first : first + LANES], coll_ref.at[side], lat, to_lon)
    for side, to_lat, top, wide in ((0, north, rows - 8, rows - 16), (1, south, 0, 0)):
        for edge, to_lon, ref, first in ((0, east, east_ref, cols - LANES), (1, west, west_ref, 0)):
            send(ref.at[top : top + 8], corf_ref.at[2 * side + edge], to_lat, to_lon)
            send(
                lev_ref.at[wide : wide + 16, first : first + LANES],
                corl_ref.at[2 * side + edge], to_lat, to_lon,
            )
    for copy in copies:
        copy.wait()


def exchange_halos(ids, proposals, sea, vel, levels, wind):
    members, rows, cols = sea.shape
    slabs = 4 * members
    shape = jax.ShapeDtypeStruct
    return pl.pallas_call(
        halo_kernel,
        out_shape=(
            shape((members, rows, cols), F32),
            shape((2, slabs, 8, cols), F32),
            shape((2, 16, cols), jnp.int32),
            shape((2, rows, LANES), F32),
            shape((2, rows, LANES), jnp.int32),
            shape((4, 8, LANES), F32),
            shape((4, 16, LANES), jnp.int32),
        ),
        in_specs=[SMEM, SMEM, VMEM, VMEM, VMEM, VMEM],
        out_specs=(VMEM,) * 7,
        scratch_shapes=[
            pltpu.VMEM((rows, LANES), F32),
            pltpu.VMEM((rows, LANES), F32),
            pltpu.SemaphoreType.DMA((20,)),
            pltpu.SemaphoreType.DMA((20,)),
        ],
        compiler_params=pltpu.CompilerParams(collective_id=0, has_side_effects=True),
        name="halo",
    )(ids, proposals, sea, vel, levels, wind)


def block_transposed(tile):
    block = iota((8, LANES), 1) // PW
    tile = pltpu.roll(tile, 0, 1, stride=PW, stride_axis=0)
    for bit in (1, 2, 4):
        tile = jnp.where((block & bit) != 0, pltpu.roll(tile, 8 - bit, 0), tile)
    return pltpu.roll(tile, 0, 1, stride=PW, stride_axis=0)


def ocean_kernel(
    total_rows, total_cols, n_lon, place_ref, sea_ref, vel_ref, lev_ref, frc_ref, rowf_ref, rowl_ref, colf_ref, coll_ref,
    corf_ref, corl_ref, conv_ref, sea_out, vel_out, part_out, gram_out,
    state, hu_ref, hue_ref, hv_ref, hvu_ref, patches,
):
    members, rows, cols = sea_ref.shape
    slabs = 4 * members
    height, width = rows + 16, cols + LANES
    n_tiles = height // 8
    step = pl.program_id(0)
    lat = place_ref[0]
    inner_south = lat > 0
    inner_north = lat < total_rows // rows - 1

    @pl.when(step == 0)
    def _():
        low = iota((rows, LANES), 1) < 64
        low8 = iota((8, LANES), 1) < 64

        for s in range(slabs):
            if s < members:
                own = sea_ref[s]
            elif s < 3 * members:
                own = vel_ref[s - members]
            else:
                own = frc_ref[s - 3 * members]
            state[s, 8 : rows + 8, :cols] = own
            state[s, 0:8, :cols] = jnp.where(inner_south, rowf_ref[0, s], 0.0)
            state[s, rows + 8 :, :cols] = jnp.where(inner_north, rowf_ref[1, s], 0.0)

            def side(east_of, west_of, mask):
                return jnp.where(
                    mask, pltpu.roll(east_of, (LANES - 8 * s) % LANES, 1) if s else east_of,
                    pltpu.roll(west_of, (2 * LANES - 8 - 8 * s) % LANES, 1),
                )

            state[s, 8 : rows + 8, cols:] = side(colf_ref[1], colf_ref[0], low)
            state[s, 0:8, cols:] = jnp.where(inner_south, side(corf_ref[1], corf_ref[0], low8), 0.0)
            state[s, rows + 8 :, cols:] = jnp.where(
                inner_north, side(corf_ref[3], corf_ref[2], low8), 0.0
            )

        low16 = iota((16, LANES), 1) < 64
        south = jnp.concatenate(
            [rowl_ref[0], jnp.where(low16, corl_ref[1], corl_ref[0])], axis=1
        ).astype(F32)
        south = jnp.where(inner_south, south, 0.0)
        north = jnp.concatenate(
            [rowl_ref[1], jnp.where(low16, corl_ref[3], corl_ref[2])], axis=1
        ).astype(F32)
        north = jnp.where(inner_north, north, 0.0)
        own = jnp.concatenate([lev_ref[...], jnp.where(low, coll_ref[1], coll_ref[0])], axis=1).astype(F32)
        depth = jnp.concatenate([south, own, north], axis=0) / NLEV
        hu = 0.5 * (depth + pltpu.roll(depth, 1, 1))
        hue = pltpu.roll(hu, width - 1, 1)
        hv = 0.5 * (depth + pltpu.roll(depth, 1, 0))
        hvu = pltpu.roll(hv, rows + 31, 0)
        for ref, value in ((hu_ref, hu), (hue_ref, hue), (hv_ref, hv), (hvu_ref, hvu)):
            ref[...] = value[8 : height + 8]

    sub = iota((8, width), 0)
    first, last = sub == 0, sub == 7
    keep_south = jnp.where(inner_south, 1.0, 0.0)
    keep_north = jnp.where(inner_north, 1.0, 0.0)
    inv_root = 1.0 / math.sqrt(rows // PH * (total_cols // PW))
    per_dev = STEPS * members // n_lon

    def member(m, carry):
        n_cur = state[2 * members + m, 0:8, :]
        n_roll = pltpu.roll(n_cur, 7, 0)
        g_before = es_before = None
        held = []
        for k in range(n_tiles):
            at = slice(8 * k, 8 * k + 8)
            level = state[m, at, :]
            e = state[members + m, at, :]
            n = n_cur
            row = (lat * rows + (8 * k - 8) + iota((8, LANES), 0)).astype(F32)
            cu = 0.25 * (CORI_BASE + CORI_SLOPE * (row + 0.5) / total_rows)
            cv = 0.25 * (CORI_BASE + CORI_SLOPE * row / total_rows)
            cu = jnp.concatenate([cu] * (width // LANES), axis=1)
            cv = jnp.concatenate([cv] * (width // LANES), axis=1)
            if k + 1 < n_tiles:
                n_cur = state[2 * members + m, 8 * k + 8 : 8 * k + 16, :]
                n_next = pltpu.roll(n_cur, 7, 0)
                n_up = jnp.where(last, n_next, n_roll)
                n_roll = n_next
            else:
                n_up = n_roll
            e_e = pltpu.roll(e, width - 1, 1)
            new = level - (
                (hue_ref[at, :] * e_e - hu_ref[at, :] * e) + (hvu_ref[at, :] * n_up - hv_ref[at, :] * n)
            )
            keep = {0: keep_south, n_tiles - 1: keep_north}.get(k)
            if keep is not None:
                new = new * keep
            g = GRAVITY * new
            g_w = pltpu.roll(g, 1, 1)
            g_roll = pltpu.roll(g, 1, 0)
            g_s = g_roll if k == 0 else jnp.where(first, g_before, g_roll)
            g_before = g_roll
            ns = n + n_up
            v_sum = ns + pltpu.roll(ns, 1, 1)
            es = e + e_e
            es_roll = pltpu.roll(es, 1, 0)
            u_sum = es + (es_roll if k == 0 else jnp.where(first, es_before, es_roll))
            es_before = es_roll
            e_new = (1.0 - DRAG_RATE) * e + (cu * v_sum - (g - g_w) + state[3 * members + m, at, :])
            n_new = (1.0 - DRAG_RATE) * n - (cv * u_sum + (g - g_s))
            if keep is not None:
                e_new = e_new * keep
                n_new = n_new * keep
            state[m, at, :] = new
            state[members + m, at, :] = e_new
            state[2 * members + m, at, :] = n_new
            if 0 < k < n_tiles - 1:
                held.append(
                    [block_transposed(new[:, c * LANES : (c + 1) * LANES]) for c in range(cols // LANES)]
                )
                if len(held) == 2:
                    for c in range(cols // LANES):
                        i = (k // 2 - 1) * (cols // LANES) + c
                        patches[16 * i : 16 * i + 16, :] = jnp.concatenate(
                            [held[0][c], held[1][c]], axis=0
                        ).astype(BF16)
                    held = []

        cells = patches[...]
        act = jnp.tanh(jnp.dot(cells, conv_ref[...], preferred_element_type=F32))
        total = jnp.sum(act, axis=0, keepdims=True) * inv_root
        item = step * members + m
        part_out[item // per_dev, pl.ds(lax.rem(item, per_dev), 1), :] = total
        slope = 1.0 - act * act
        high = slope.astype(BF16)
        rest = (slope - high.astype(F32)).astype(BF16)
        over_rows = (((0,), (0,)), ((), ()))
        gram_out[m] = lax.dot_general(
            cells, high, over_rows, preferred_element_type=F32
        ) + lax.dot_general(cells, rest, over_rows, preferred_element_type=F32)
        return carry

    lax.fori_loop(0, members, member, 0)

    @pl.when(step == STEPS - 1)
    def _():
        for s in range(members):
            sea_out[s] = state[s, 8 : rows + 8, :cols]
        for s in range(2 * members):
            vel_out[s] = state[members + s, 8 : rows + 8, :cols]


def run_ocean(n_lon, n_lat, place, sea, vel, levels, halos, conv):
    members, rows, cols = sea.shape
    feat = conv.shape[1]
    height, width = rows + 16, cols + LANES
    per_dev = STEPS * members // n_lon
    shape = jax.ShapeDtypeStruct

    def whole(x):
        return pl.BlockSpec(x.shape, lambda t, *_: (0,) * len(x.shape), pipeline_mode=pl.Buffered(1))

    operands = (sea, vel, levels) + tuple(halos) + (conv,)
    outs = (
        shape(sea.shape, F32),
        shape(vel.shape, F32),
        shape((n_lon, per_dev, feat), F32),
        shape((STEPS * members, PH * PW, feat), F32),
    )
    return pl.pallas_call(
        functools.partial(ocean_kernel, rows * n_lat, cols * n_lon, n_lon),
        out_shape=outs,
        grid_spec=pltpu.PrefetchScalarGridSpec(
            num_scalar_prefetch=1,
            grid=(STEPS,),
            in_specs=[whole(x) for x in operands],
            out_specs=(
                whole(outs[0]),
                whole(outs[1]),
                whole(outs[2]),
                pl.BlockSpec((members, PH * PW, feat), lambda t, *_: (t, 0, 0)),
            ),
            scratch_shapes=[pltpu.VMEM((4 * members, height, width), F32)]
            + [pltpu.VMEM((height, width), F32)] * 4
            + [pltpu.VMEM((rows // PH * (cols // PW), PH * PW), BF16)],
        ),
        compiler_params=pltpu.CompilerParams(dimension_semantics=("arbitrary",)),
        name="ocean",
    )(place, *operands)


def precise(a, b, dims=(((1,), (0,)), ((), ()))):
    return lax.dot_general(a, b, dims, precision=PRECISE, preferred_element_type=F32)


def flow_gradients(params, summ, w_low, w_sum, b_in, w_out, b_out):
    lane = iota(params.shape, 1)
    hidden = jnp.tanh(precise(params, w_low) + precise(summ, w_sum) + b_in)
    raw = precise(hidden, w_out) + b_out
    log_scale = jnp.tanh(raw)
    scaled = pltpu.roll(params, LANES - HALF, 1) * jnp.exp(log_scale)
    latent = scaled + pltpu.roll(raw, LANES - HALF, 1)
    d_scale = (latent * scaled - 1.0) * (1.0 - log_scale * log_scale)
    d_raw = jnp.where(
        lane < HALF, d_scale, jnp.where(lane < 2 * HALF, pltpu.roll(latent, HALF, 1), 0.0)
    )
    d_hidden = precise(d_raw, w_out, (((1,), (1,)), ((), ()))) * (1.0 - hidden * hidden)
    return hidden, d_raw, d_hidden


def learn_kernel(
    inv_root, flat_size, ids_ref, prop_ref, part_ref, gram_ref, w_in_ref, b_in_ref, w_out_ref, b_out_ref, summary_ref, flat_ref,
    prop_pad, w_low, w_sum, w_out_pad, b_out_pad, near_sum, own_sum, lon_sum, all_sum, ds_ref,
    near_grad, got_grad, mid_own, mid_grad, end_own, end_grad, out_pad,
    send_sem, recv_sem,
):
    n_lon, per_dev, feat = part_ref.shape
    hid = w_in_ref.shape[1]
    n_lat, n_grp = lax.axis_size("lat"), lax.axis_size("grp")
    n_plane = n_lat * n_grp
    n_items = n_lon * per_dev
    n_members = prop_ref.shape[0]
    members = n_members // n_grp
    slice_rows = near_grad.shape[1]
    lon, lat, grp = lax.axis_index("lon"), lax.axis_index("lat"), lax.axis_index("grp")
    plane = lat * n_grp + grp

    def lon_peer(d):
        to = lax.rem(lon + d, n_lon)
        return to, {"lon": to}

    def plane_peer(d):
        to = lax.rem(plane + d, n_plane)
        return to, {"lat": to // n_grp, "grp": lax.rem(to, n_grp)}

    barrier = pltpu.get_barrier_semaphore()

    def greet(peer):
        def body(d, carry):
            pl.semaphore_signal(barrier, inc=1, device_id=peer(d)[1], device_id_type=MESH)
            return carry

        return body

    lax.fori_loop(1, n_lon, greet(lon_peer), 0)
    lax.fori_loop(1, n_plane, greet(plane_peer), 0)

    prop_pad[...] = jnp.zeros_like(prop_pad)
    prop_pad[:, : prop_ref.shape[1]] = prop_ref[...]
    w_low[...] = jnp.zeros_like(w_low)
    w_low[:HALF] = w_in_ref[:HALF]
    w_sum[...] = w_in_ref[HALF:]
    w_out_pad[...] = jnp.zeros_like(w_out_pad)
    w_out_pad[:, : 2 * HALF] = w_out_ref[...]
    b_out_pad[...] = jnp.zeros_like(b_out_pad)
    b_out_pad[:, : 2 * HALF] = b_out_ref[...]
    b_in, b_out = b_in_ref[...], b_out_pad[...]
    pick = (iota((n_members, n_members), 0) == ids_ref[...]).astype(F32)
    member_params = precise(pick, prop_pad[...], (((0,), (0,)), ((), ())))

    def params_of(n, group):
        inner = lax.rem(n, n_items)
        item = lax.rem(inner, n_lon) * per_dev + inner // n_lon
        chosen = group * members + lax.rem(item, members)
        return precise((chosen == iota(n.shape, 1)).astype(F32), member_params)

    n_near = iota((n_items, n_members), 0)
    near_params = params_of(n_near, grp)
    n_all = iota((n_plane * n_items, n_members), 0)
    all_params = params_of(n_all, lax.rem(n_all // n_items, n_grp))

    pl.semaphore_wait(barrier, n_lon + n_plane - 2)

    def exchange(phase, count, peer, source, target):
        def copy(d):
            to, device = peer(d)
            return pltpu.make_async_remote_copy(
                src_ref=source(to), dst_ref=target(d), send_sem=send_sem.at[phase, d],
                recv_sem=recv_sem.at[phase, d], device_id=device, device_id_type=MESH,
            )

        def start(d, carry):
            copy(d).start()
            return carry

        def finish(d, carry):
            copy(d).wait()
            return carry

        lax.fori_loop(1, count, start, 0)
        return lambda: lax.fori_loop(1, count, finish, 0)

    wait = exchange(0, n_lon, lon_peer, lambda to: part_ref.at[to], lambda d: near_sum.at[d])
    near_sum[0] = part_ref[lon]
    wait()
    total = near_sum[0]
    for d in range(1, n_lon):
        total = total + near_sum[d]
    own_sum[...] = total
    summary_ref[...] = total
    wait = exchange(1, n_lon, lon_peer, lambda to: own_sum, lambda d: lon_sum.at[lon])
    lon_sum[lon] = total
    wait()
    near = jnp.concatenate([lon_sum[:, q, :] for q in range(per_dev)], axis=0)
    all_sum[plane] = near
    wait_all = exchange(
        2, n_plane, plane_peer, lambda to: all_sum.at[plane], lambda d: all_sum.at[plane]
    )

    _, _, d_hidden = flow_gradients(near_params, near, w_low[...], w_sum[...], b_in, w_out_pad[...], b_out)
    ds_ref[...] = precise(d_hidden, w_sum[...], (((1,), (1,)), ((), ()))) * inv_root

    def accumulate(n, total):
        item = lax.rem(n, n_lon) * per_dev + n // n_lon
        return total + gram_ref[item] * ds_ref[pl.ds(n, 1), :]

    conv_grad = lax.fori_loop(0, n_items, accumulate, jnp.zeros(gram_ref.shape[1:], F32))
    near_grad[...] = conv_grad.reshape(near_grad.shape)
    wait = exchange(3, n_lon, lon_peer, lambda to: near_grad.at[to], lambda d: got_grad.at[d])

    wait_all()
    summ = all_sum[...].reshape(n_plane * n_items, feat)
    hidden, d_raw, d_hidden = flow_gradients(
        all_params, summ, w_low[...], w_sum[...], b_in, w_out_pad[...], b_out
    )

    got_grad[0] = near_grad[lon]
    wait()
    total = got_grad[0]
    for d in range(1, n_lon):
        total = total + got_grad[d]
    mid_own[...] = total
    wait = exchange(4, n_plane, plane_peer, lambda to: mid_own, lambda d: mid_grad.at[plane])
    mid_grad[plane] = total

    over_rows = (((0,), (0,)), ((), ()))
    conv_rows = PH * PW * feat // LANES
    wide = hid // LANES
    flat_ref[...] = jnp.zeros_like(flat_ref)
    g_low = precise(all_params, d_hidden, over_rows)[:HALF]
    g_sum = precise(summ, d_hidden, over_rows)
    for h in range(wide):
        flat_ref[pl.ds(conv_rows + h, HALF, stride=wide), :] = g_low[:, h * LANES : (h + 1) * LANES]
        flat_ref[pl.ds(conv_rows + HALF * wide + h, feat, stride=wide), :] = g_sum[:, h * LANES : (h + 1) * LANES]

    wait()
    total = mid_grad[0]
    for d in range(1, n_plane):
        total = total + mid_grad[d]
    end_own[...] = total
    wait = exchange(5, n_lon, lon_peer, lambda to: end_own, lambda d: end_grad.at[lon])
    end_grad[lon] = total

    base = conv_rows + (HALF + feat) * wide
    g_b_in = jnp.sum(d_hidden, axis=0, keepdims=True)
    for h in range(wide):
        flat_ref[base + h : base + h + 1, :] = g_b_in[:, h * LANES : (h + 1) * LANES]
    base += wide
    out_pad[...] = precise(hidden, d_raw, over_rows)
    per_row = LANES // (2 * HALF)
    out_rows = hid // per_row
    packed = out_pad[pl.ds(0, out_rows, stride=per_row), :]
    for s in range(1, per_row):
        packed = packed + pltpu.roll(
            out_pad[pl.ds(s, out_rows, stride=per_row), :], s * 2 * HALF, 1
        )
    flat_ref[base : base + out_rows, :] = packed
    base += out_rows
    flat_ref[base : base + 1, :] = jnp.sum(d_raw, axis=0, keepdims=True)

    wait()
    conv_grad = end_grad[...].reshape(PH * PW, feat)
    halves = feat // LANES
    for h in range(halves):
        flat_ref[pl.ds(h, PH * PW, stride=halves), :] = conv_grad[:, h * LANES : (h + 1) * LANES]
    flat = flat_ref[...]
    mean = jnp.sum(jnp.sum(flat * flat, axis=0, keepdims=True), axis=1, keepdims=True) / flat_size
    flat_ref[...] = flat * (-1.0 / jnp.sqrt(mean + EPSILON))


def learn(inv_root, ids, proposals, part, gram, w_in, b_in, w_out, b_out):
    n_lon, per_dev, feat = part.shape
    hid = w_in.shape[1]
    n_plane = lax.axis_size("lat") * lax.axis_size("grp")
    n_items = n_lon * per_dev
    cells = gram.shape[1]
    flat_size = cells * feat + w_in.size + b_in.size + w_out.size + b_out.size
    flat_rows = -(-flat_size // (8 * LANES)) * 8
    slice_rows = cells // n_lon
    piece = (slice_rows, feat)
    summary, flat = pl.pallas_call(
        functools.partial(learn_kernel, inv_root, float(flat_size)),
        out_shape=(
            jax.ShapeDtypeStruct((per_dev, feat), F32),
            jax.ShapeDtypeStruct((flat_rows, LANES), F32),
        ),
        in_specs=[VMEM] * 8,
        out_specs=(VMEM, VMEM),
        scratch_shapes=[
            pltpu.VMEM((proposals.shape[0], LANES), F32),
            pltpu.VMEM((LANES, hid), F32),
            pltpu.VMEM((feat, hid), F32),
            pltpu.VMEM((hid, LANES), F32),
            pltpu.VMEM((1, LANES), F32),
            pltpu.VMEM((n_lon, per_dev, feat), F32),
            pltpu.VMEM((per_dev, feat), F32),
            pltpu.VMEM((n_lon, per_dev, feat), F32),
            pltpu.VMEM((n_plane, n_items, feat), F32),
            pltpu.VMEM((n_items, feat), F32),
            pltpu.VMEM((n_lon,) + piece, F32),
            pltpu.VMEM((n_lon,) + piece, F32),
            pltpu.VMEM(piece, F32),
            pltpu.VMEM((n_plane,) + piece, F32),
            pltpu.VMEM(piece, F32),
            pltpu.VMEM((n_lon,) + piece, F32),
            pltpu.VMEM((hid, LANES), F32),
            pltpu.SemaphoreType.DMA((6, max(n_lon, n_plane))),
            pltpu.SemaphoreType.DMA((6, max(n_lon, n_plane))),
        ],
        compiler_params=pltpu.CompilerParams(collective_id=1, has_side_effects=True),
        name="learn",
    )(ids.reshape(1, -1), proposals, part, gram, w_in, b_in.reshape(1, -1), w_out, b_out.reshape(1, -1))
    return summary, flat.reshape(-1)[:flat_size]


def shards(
    sea_surface, velocity, levels, wind_basis, proposals, member_ids, conv_weight,
    couple_in, couple_in_bias, couple_out, couple_out_bias,
):
    members, rows, cols = sea_surface.shape
    n_lon, n_lat = lax.axis_size("lon"), lax.axis_size("lat")
    vel = velocity.reshape(2 * members, rows, cols)
    frc, *received = exchange_halos(member_ids, proposals, sea_surface, vel, levels, wind_basis)
    place = jnp.stack([lax.axis_index("lat"), lax.axis_index("lon")]).astype(jnp.int32)
    sea_out, vel_out, part, gram = run_ocean(
        n_lon, n_lat, place, sea_surface, vel, levels, (frc, *received), conv_weight
    )
    inv_root = 1.0 / math.sqrt(rows // PH * (cols * n_lon // PW))
    summary, weight_step = learn(
        inv_root, member_ids, proposals, part, gram, couple_in, couple_in_bias, couple_out, couple_out_bias
    )
    return (
        sea_out,
        vel_out.reshape(velocity.shape),
        summary.reshape((1, 1, 1) + summary.shape),
        weight_step,
    )


def solution(mesh):
    in_specs = (
        P("grp", "lat", "lon"),
        P(None, "grp", "lat", "lon"),
        P("lat", "lon"),
        P(None, "lat", "lon"),
        P(), P(), P(), P(), P(), P(), P(),
    )
    out_specs = (
        P("grp", "lat", "lon"),
        P(None, "grp", "lat", "lon"),
        P("lon", "lat", "grp", None, None),
        P(),
    )
    return jax.shard_map(shards, mesh=mesh, in_specs=in_specs, out_specs=out_specs, check_vma=False)
```

```python
import functools
import math

import jax
import jax.numpy as jnp
from jax import lax
from jax.experimental import pallas as pl
from jax.experimental.pallas import tpu as pltpu
from jax.sharding import PartitionSpec as P

STEPS = 8
NLEV = 50
PH = 8
PW = 16
GRAVITY = 0.45
DRAG_RATE = 0.02
CORI_BASE = 0.05
CORI_SLOPE = 0.1
WIND_SCALE = 0.05
EPSILON = 1e-06
HALF = 8
LANES = 128
F32 = jnp.float32
BF16 = jnp.bfloat16
PRECISE = lax.Precision.HIGHEST
MESH = pl.DeviceIdType.MESH
ANY = pl.BlockSpec(memory_space=pl.ANY)
VMEM = pl.BlockSpec(memory_space=pltpu.VMEM)
SMEM = pl.BlockSpec(memory_space=pltpu.SMEM)


def iota(shape, dim):
    return lax.broadcasted_iota(jnp.int32, shape, dim)


def block_transposed(tile):
    block = iota((8, LANES), 1) // PW
    tile = pltpu.roll(tile, 0, 1, stride=PW, stride_axis=0)
    for bit in (1, 2, 4):
        tile = jnp.where((block & bit) != 0, pltpu.roll(tile, 8 - bit, 0), tile)
    return pltpu.roll(tile, 0, 1, stride=PW, stride_axis=0)


def precise(a, b, dims=(((1,), (0,)), ((), ()))):
    return lax.dot_general(a, b, dims, precision=PRECISE, preferred_element_type=F32)


ROWS_OVER = (((0,), (0,)), ((), ()))
COLS_OVER = (((1,), (1,)), ((), ()))


def flow_gradients(params, summ, w_low, w_sum, b_in, w_out, b_out):
    lane = iota(params.shape, 1)
    hidden = jnp.tanh(precise(params, w_low) + precise(summ, w_sum) + b_in)
    raw = precise(hidden, w_out, COLS_OVER) + b_out
    log_scale = jnp.tanh(raw)
    scaled = pltpu.roll(params, LANES - HALF, 1) * jnp.exp(log_scale)
    latent = scaled + pltpu.roll(raw, LANES - HALF, 1)
    d_scale = (latent * scaled - 1.0) * (1.0 - log_scale * log_scale)
    d_raw = jnp.where(
        lane < HALF, d_scale, jnp.where(lane < 2 * HALF, pltpu.roll(latent, HALF, 1), 0.0)
    )
    d_hidden = precise(d_raw, w_out) * (1.0 - hidden * hidden)
    return hidden, d_raw, d_hidden


LEVEL, EAST, NORTH, FORCE = range(4)


def main_kernel(
    n_z, ids_s, prop_s, ids_ref, prop_ref, lev_ref, conv_ref, w_in_ref, b_in_ref, w_out_ref, b_out_ref,
    sea_ref, vel_ref, wind_ref,
    summary_ref, flat_ref, sea_out, vel_out,
    state, wind, hu_ref, hue_ref, hv_ref, hvu_ref, patches, gram, east_pack, west_pack,
    rowl_ref, colf_ref, coll_ref, corf_ref, corl_ref,
    prop_pad, w_low, w_sum, w_out_pad, b_out_pad, near_par, part, parts, all_sum, ds_ref,
    near_grad, got_grad, mid_grad, end_grad, out_pad,
    load_sem, store_sem, row_send, row_recv, edge_send, edge_recv, part_send, part_recv, sum_send, sum_recv,
    grad_send, grad_recv,
):
    members, _, height, width = state.shape
    rows, cols = height - 16, width - LANES
    n_lon, n_lat, n_grp = lax.axis_size("lon"), lax.axis_size("lat"), lax.axis_size("grp")
    lon, lat, grp = lax.axis_index("lon"), lax.axis_index("lat"), lax.axis_index("grp")
    total_rows, total_cols = rows * n_lat, cols * n_lon
    n_plane, n_hi = n_lat * n_grp, n_lon // n_z
    n_wide = n_hi * n_plane
    plane = lat * n_grp + grp
    hi, z = lon // n_z, lax.rem(lon, n_z)
    wide = hi * n_plane + plane
    n_members = prop_ref.shape[0]
    n_items = members * STEPS
    per_dev = n_items // n_lon
    feat = conv_ref.shape[1]
    hid = w_in_ref.shape[1]
    inv_root = 1.0 / math.sqrt(rows // PH * (total_cols // PW))
    own_rows, own_cols = slice(8, rows + 8), slice(0, cols)

    def lon_peer(d):
        to = lax.rem(lon + d, n_lon)
        return to, {"lon": to}

    def plane_peer(d):
        to = lax.rem(plane + d, n_plane)
        return to, {"lat": to // n_grp, "grp": lax.rem(to, n_grp)}

    def z_peer(d):
        to = lax.rem(z + d, n_z)
        return to, {"lon": hi * n_z + to}

    def wide_peer(d):
        to = lax.rem(wide + d, n_wide)
        rest = lax.rem(to, n_plane)
        return to, {"lon": (to // n_plane) * n_z + z, "lat": rest // n_grp, "grp": lax.rem(rest, n_grp)}

    east, west = lax.rem(lon + 1, n_lon), lax.rem(lon + n_lon - 1, n_lon)
    north, south = lax.rem(lat + 1, n_lat), lax.rem(lat + n_lat - 1, n_lat)

    barrier = pltpu.get_barrier_semaphore()
    for to_lat in (lat, north, south):
        for to_lon in (lon, east, west):
            if to_lat is lat and to_lon is lon:
                continue
            pl.semaphore_signal(
                barrier, inc=1, device_id={"lon": to_lon, "lat": to_lat}, device_id_type=MESH
            )

    def greet(peer):
        def body(d, carry):
            pl.semaphore_signal(barrier, inc=1, device_id=peer(d)[1], device_id_type=MESH)
            return carry

        return body

    lax.fori_loop(1, n_lon, greet(lon_peer), 0)
    lax.fori_loop(1, n_wide, greet(wide_peer), 0)

    loads = [
        pltpu.make_async_copy(wind_ref, wind, load_sem.at[0]),
        pltpu.make_async_copy(sea_ref, state.at[:, LEVEL, own_rows, own_cols], load_sem.at[1]),
        pltpu.make_async_copy(vel_ref.at[0], state.at[:, EAST, own_rows, own_cols], load_sem.at[2]),
        pltpu.make_async_copy(vel_ref.at[1], state.at[:, NORTH, own_rows, own_cols], load_sem.at[3]),
    ]
    for load in loads:
        load.start()

    coeffs = []
    for m in range(members):
        row = ids_s[grp * members + m]
        for k in range(wind_ref.shape[0]):
            full = prop_s[row, k]
            scaled = full * 65537.0
            coeffs.append(scaled - (scaled - full))

    loads[0].wait()

    def force(r, carry):
        at = pl.ds(pl.multiple_of(r * 16, 16), 16)
        total = [None] * members
        for k in range(wind_ref.shape[0]):
            blow = wind[k, at, :].astype(F32)
            for m in range(members):
                term = coeffs[m * wind_ref.shape[0] + k] * blow
                total[m] = term if k == 0 else total[m] + term
        for m in range(members):
            state[m, FORCE, pl.ds(pl.multiple_of(r * 16 + 8, 8), 16), own_cols] = WIND_SCALE * total[m]
        return carry

    lax.fori_loop(0, rows // 16, force, 0)
    for load in loads[1:]:
        load.wait()

    slot = iota((rows, LANES), 1) // 8
    east_edge = jnp.zeros((rows, LANES), F32)
    west_edge = jnp.zeros((rows, LANES), F32)
    for m in range(members):
        for f in range(4):
            s = 4 * m + f
            right = state[m, f, own_rows, cols - LANES : cols]
            left = state[m, f, own_rows, :LANES]
            east_edge = jnp.where(slot == s, pltpu.roll(right, (8 * s + 8) % LANES, 1), east_edge)
            west_edge = jnp.where(slot == s, pltpu.roll(left, 8 * s, 1) if s else left, west_edge)
    east_pack[...] = east_edge
    west_pack[...] = west_edge

    pl.semaphore_wait(barrier, 8 + n_lon - 1 + n_wide - 1)

    edges = []

    def send(src, dst, to_lat, to_lon):
        i = len(edges)
        copy = pltpu.make_async_remote_copy(
            src_ref=src, dst_ref=dst, send_sem=edge_send.at[i], recv_sem=edge_recv.at[i],
            device_id={"lon": to_lon, "lat": to_lat}, device_id_type=MESH,
        )
        copy.start()
        edges.append(copy)

    def row_copy(m, side):
        return pltpu.make_async_remote_copy(
            src_ref=state.at[m, :, (slice(rows, rows + 8), slice(8, 16))[side], own_cols],
            dst_ref=state.at[m, :, (slice(0, 8), slice(rows + 8, rows + 16))[side], own_cols],
            send_sem=row_send.at[m, side], recv_sem=row_recv.at[m, side],
            device_id={"lat": (north, south)[side]}, device_id_type=MESH,
        )

    for side, to_lat, wide_rows in ((0, north, slice(rows - 16, rows)), (1, south, slice(0, 16))):
        send(lev_ref.at[wide_rows], rowl_ref.at[side], to_lat, lon)
    for side, to_lon, ref, first in ((0, east, east_pack, cols - LANES), (1, west, west_pack, 0)):
        send(ref, colf_ref.at[side], lat, to_lon)
        send(lev_ref.at[:, first : first + LANES], coll_ref.at[side], lat, to_lon)
    for side in (0, 1):
        row_copy(0, side).start()
    for side, to_lat, top, wide_rows in (
        (0, north, rows - 8, slice(rows - 16, rows)), (1, south, 0, slice(0, 16)),
    ):
        for edge, to_lon, ref, first in ((0, east, east_pack, cols - LANES), (1, west, west_pack, 0)):
            send(ref.at[top : top + 8], corf_ref.at[2 * side + edge], to_lat, to_lon)
            send(
                lev_ref.at[wide_rows, first : first + LANES], corl_ref.at[2 * side + edge], to_lat, to_lon
            )
    for m in range(1, members):
        for side in (0, 1):
            row_copy(m, side).start()

    prop_pad[...] = jnp.zeros_like(prop_pad)
    prop_pad[:, : prop_ref.shape[1]] = prop_ref[...]
    w_low[...] = jnp.zeros_like(w_low)
    w_low[:HALF] = w_in_ref[:HALF]
    w_sum[...] = w_in_ref[HALF:]
    w_out_pad[...] = jnp.zeros_like(w_out_pad)
    w_out_pad[: 2 * HALF] = w_out_ref[...]
    b_out_pad[...] = jnp.zeros_like(b_out_pad)
    b_out_pad[:, : 2 * HALF] = b_out_ref[...]
    b_in, b_out = b_in_ref[...], b_out_pad[...]
    pick = (iota((n_members, n_members), 0) == ids_ref[...]).astype(F32)
    member_params = precise(pick, prop_pad[...], ROWS_OVER)

    def params_of(n, group):
        chosen = group * members + lax.rem(n, n_items) // STEPS
        return precise((chosen == iota(n.shape, 1)).astype(F32), member_params)

    near_par[...] = params_of(iota((n_items, n_members), 0), grp)

    for copy in edges:
        copy.wait()

    inner_south, inner_north = lat > 0, lat < n_lat - 1
    low = iota((rows, LANES), 1) < 64
    low8 = iota((8, LANES), 1) < 64
    for m in range(members):
        for f in range(4):
            s = 4 * m + f

            def beyond(east_of, west_of, mask):
                return jnp.where(
                    mask, pltpu.roll(east_of, (LANES - 8 * s) % LANES, 1) if s else east_of,
                    pltpu.roll(west_of, (2 * LANES - 8 - 8 * s) % LANES, 1),
                )

            state[m, f, own_rows, cols:] = beyond(colf_ref[1], colf_ref[0], low)
            state[m, f, 0:8, cols:] = beyond(corf_ref[1], corf_ref[0], low8)
            state[m, f, rows + 8 :, cols:] = beyond(corf_ref[3], corf_ref[2], low8)

    low16 = iota((16, LANES), 1) < 64
    below = jnp.concatenate([rowl_ref[0], jnp.where(low16, corl_ref[1], corl_ref[0])], axis=1).astype(F32)
    above = jnp.concatenate([rowl_ref[1], jnp.where(low16, corl_ref[3], corl_ref[2])], axis=1).astype(F32)
    own = jnp.concatenate([lev_ref[...], jnp.where(low, coll_ref[1], coll_ref[0])], axis=1).astype(F32)
    depth = jnp.concatenate(
        [jnp.where(inner_south, below, 0.0), own, jnp.where(inner_north, above, 0.0)], axis=0
    ) / NLEV
    hu = 0.5 * (depth + pltpu.roll(depth, 1, 1))
    hv = 0.5 * (depth + pltpu.roll(depth, 1, 0))
    for ref, value in (
        (hu_ref, hu), (hue_ref, pltpu.roll(hu, width - 1, 1)),
        (hv_ref, hv), (hvu_ref, pltpu.roll(hv, rows + 31, 0)),
    ):
        ref[...] = value[8 : height + 8]

    sub = iota((8, width), 0)
    first, last = sub == 0, sub == 7
    keep_south = jnp.where(inner_south, 1.0, 0.0)
    keep_north = jnp.where(inner_north, 1.0, 0.0)
    n_tiles = height // 8

    def advance(m, step):
        n_cur = state[m, NORTH, 0:8, :]
        n_roll = pltpu.roll(n_cur, 7, 0)
        g_before = es_before = None
        held = []
        for k in range(n_tiles):
            at = slice(8 * k, 8 * k + 8)
            e = state[m, EAST, at, :]
            n = n_cur
            row = (lat * rows + (8 * k - 8) + iota((8, LANES), 0)).astype(F32)
            cu = 0.25 * (CORI_BASE + CORI_SLOPE * (row + 0.5) / total_rows)
            cv = 0.25 * (CORI_BASE + CORI_SLOPE * row / total_rows)
            cu = jnp.concatenate([cu] * (width // LANES), axis=1)
            cv = jnp.concatenate([cv] * (width // LANES), axis=1)
            if k + 1 < n_tiles:
                n_cur = state[m, NORTH, 8 * k + 8 : 8 * k + 16, :]
                n_next = pltpu.roll(n_cur, 7, 0)
                n_up = jnp.where(last, n_next, n_roll)
                n_roll = n_next
            else:
                n_up = n_roll
            e_e = pltpu.roll(e, width - 1, 1)
            new = state[m, LEVEL, at, :] - (
                (hue_ref[at, :] * e_e - hu_ref[at, :] * e) + (hvu_ref[at, :] * n_up - hv_ref[at, :] * n)
            )
            keep = {0: keep_south, n_tiles - 1: keep_north}.get(k)
            if keep is not None:
                new = new * keep
            g = GRAVITY * new
            g_w = pltpu.roll(g, 1, 1)
            g_roll = pltpu.roll(g, 1, 0)
            g_s = g_roll if k == 0 else jnp.where(first, g_before, g_roll)
            g_before = g_roll
            ns = n + n_up
            v_sum = ns + pltpu.roll(ns, 1, 1)
            es = e + e_e
            es_roll = pltpu.roll(es, 1, 0)
            u_sum = es + (es_roll if k == 0 else jnp.where(first, es_before, es_roll))
            es_before = es_roll
            e_new = (1.0 - DRAG_RATE) * e + (cu * v_sum - (g - g_w) + state[m, FORCE, at, :])
            n_new = (1.0 - DRAG_RATE) * n - (cv * u_sum + (g - g_s))
            if keep is not None:
                e_new = e_new * keep
                n_new = n_new * keep
            state[m, LEVEL, at, :] = new
            state[m, EAST, at, :] = e_new
            state[m, NORTH, at, :] = n_new
            if 0 < k < n_tiles - 1:
                held.append(
                    [block_transposed(new[:, c * LANES : (c + 1) * LANES]) for c in range(cols // LANES)]
                )
                if len(held) == 2:
                    for c in range(cols // LANES):
                        i = (k // 2 - 1) * (cols // LANES) + c
                        patches[16 * i : 16 * i + 16, :] = jnp.concatenate(
                            [held[0][c], held[1][c]], axis=0
                        ).astype(BF16)
                    held = []

        cells = patches[...]
        act = jnp.tanh(jnp.dot(cells, conv_ref[...], preferred_element_type=F32))
        item = m * STEPS + step
        part[pl.ds(item, 1), :] = jnp.sum(act, axis=0, keepdims=True) * inv_root
        slope = 1.0 - act * act
        high = slope.astype(BF16)
        rest = (slope - high.astype(F32)).astype(BF16)
        gram[item] = lax.dot_general(
            cells, high, ROWS_OVER, preferred_element_type=F32
        ) + lax.dot_general(cells, rest, ROWS_OVER, preferred_element_type=F32)

    def exchange(count, peer, source, target, sends, recvs):
        def copy(d):
            to, device = peer(d)
            return pltpu.make_async_remote_copy(
                src_ref=source(to), dst_ref=target(d), send_sem=sends.at[d],
                recv_sem=recvs.at[d], device_id=device, device_id_type=MESH,
            )

        def start(d, carry):
            copy(d).start()
            return carry

        def finish(d, carry):
            copy(d).wait()
            return carry

        return (
            lambda: lax.fori_loop(1, count, start, 0),
            lambda: lax.fori_loop(1, count, finish, 0),
        )

    def group(m):
        return pl.ds(pl.multiple_of(m * STEPS, STEPS), STEPS)

    def share_parts(m):
        return exchange(
            n_lon, lon_peer, lambda to: part.at[group(m)], lambda d: parts.at[lon, group(m)],
            part_send.at[m], part_recv.at[m],
        )

    def share_sums(m):
        return exchange(
            n_plane, plane_peer, lambda to: all_sum.at[plane, group(m)], lambda d: all_sum.at[plane, group(m)],
            sum_send.at[m], sum_recv.at[m],
        )

    def summarize(m):
        share_parts(m)[1]()
        total = parts[0, group(m), :]
        for other in range(1, n_lon):
            total = total + parts[other, group(m), :]
        all_sum[plane, group(m), :] = total
        share_sums(m)[0]()

    def stores(m):
        own = (own_rows, own_cols)
        return [
            pltpu.make_async_copy(state.at[(m, LEVEL) + own], sea_out.at[m], store_sem.at[m, 0]),
            pltpu.make_async_copy(state.at[(m, EAST) + own], vel_out.at[0, m], store_sem.at[m, 1]),
            pltpu.make_async_copy(state.at[(m, NORTH) + own], vel_out.at[1, m], store_sem.at[m, 2]),
        ]

    def member(m, carry):
        for side in (0, 1):
            row_copy(m, side).wait()

        @pl.when(lat == 0)
        def _():
            state[m, :, 0:8, :] = jnp.zeros((4, 8, width), F32)

        @pl.when(lat == n_lat - 1)
        def _():
            state[m, :, rows + 8 :, :] = jnp.zeros((4, 8, width), F32)

        def one(step, inner):
            advance(m, step)
            return inner

        lax.fori_loop(0, STEPS, one, 0)
        for store in stores(m):
            store.start()
        parts[lon, group(m), :] = part[group(m), :]
        share_parts(m)[0]()

        @pl.when(m > 0)
        def _():
            summarize(m - 1)

        return carry

    lax.fori_loop(0, members, member, 0)

    def slopes(first_row, end_row, total):
        at = slice(first_row, end_row)
        _, _, d_hidden = flow_gradients(
            near_par[at], all_sum[plane, at, :], w_low[...], w_sum[...], b_in, w_out_pad[...], b_out
        )
        ds_ref[at] = precise(d_hidden, w_sum[...], COLS_OVER) * inv_root
        return lax.fori_loop(
            first_row, end_row, lambda j, acc: acc + gram[j] * ds_ref[pl.ds(j, 1), :], total
        )

    final = (members - 1) * STEPS
    conv_grad = slopes(0, final, jnp.zeros(gram.shape[1:], F32))
    summarize(members - 1)
    conv_grad = slopes(final, n_items, conv_grad)
    halves = feat // LANES
    for i in range(PH * PW // 8):
        for h in range(halves):
            near_grad[i * halves + h] = conv_grad[8 * i : 8 * i + 8, h * LANES : (h + 1) * LANES]
    per = near_grad.shape[0] // n_wide
    start, finish = exchange(
        n_wide, wide_peer, lambda to: near_grad.at[pl.ds(to * per, per)], lambda d: got_grad.at[d],
        grad_send.at[0], grad_recv.at[0],
    )
    start()

    for q in range(per_dev):
        item = lon * per_dev + q
        summary_ref[q : q + 1, :] = all_sum[
            plane, pl.ds(lax.rem(item, members) * STEPS + item // members, 1), :
        ]

    for m in range(members):
        share_sums(m)[1]()
    n_all = iota((n_plane * n_items, n_members), 0)
    all_params = params_of(n_all, lax.rem(n_all // n_items, n_grp))
    summ = all_sum[...].reshape(n_plane * n_items, feat)
    hidden, d_raw, d_hidden = flow_gradients(
        all_params, summ, w_low[...], w_sum[...], b_in, w_out_pad[...], b_out
    )

    got_grad[0] = near_grad[pl.ds(wide * per, per)]
    finish()
    total = got_grad[0]
    for d in range(1, n_wide):
        total = total + got_grad[d]
    mid_grad[z] = total
    start, finish = exchange(
        n_z, z_peer, lambda to: mid_grad.at[z], lambda d: mid_grad.at[z], grad_send.at[1], grad_recv.at[1]
    )
    start()

    conv_rows = PH * PW * feat // LANES
    w_cols = hid // LANES
    flat_ref[...] = jnp.zeros_like(flat_ref)
    g_low = precise(all_params, d_hidden, ROWS_OVER)[:HALF]
    g_sum = precise(summ, d_hidden, ROWS_OVER)
    for h in range(w_cols):
        flat_ref[pl.ds(conv_rows + h, HALF, stride=w_cols), :] = g_low[:, h * LANES : (h + 1) * LANES]
        flat_ref[pl.ds(conv_rows + HALF * w_cols + h, feat, stride=w_cols), :] = g_sum[
            :, h * LANES : (h + 1) * LANES
        ]

    finish()
    total = mid_grad[0]
    for d in range(1, n_z):
        total = total + mid_grad[d]
    mine = pl.ds(wide * per, per)
    end_grad[mine] = total
    start, finish = exchange(
        n_wide, wide_peer, lambda to: end_grad.at[mine], lambda d: end_grad.at[mine],
        grad_send.at[2], grad_recv.at[2],
    )
    start()

    base = conv_rows + (HALF + feat) * w_cols
    g_b_in = jnp.sum(d_hidden, axis=0, keepdims=True)
    for h in range(w_cols):
        flat_ref[base + h : base + h + 1, :] = g_b_in[:, h * LANES : (h + 1) * LANES]
    base += w_cols
    out_pad[...] = precise(hidden, d_raw, ROWS_OVER)
    per_row = LANES // (2 * HALF)
    out_rows = hid // per_row
    packed = out_pad[pl.ds(0, out_rows, stride=per_row), :]
    for s in range(1, per_row):
        packed = packed + pltpu.roll(
            out_pad[pl.ds(s, out_rows, stride=per_row), :], s * 2 * HALF, 1
        )
    flat_ref[base : base + out_rows, :] = packed
    base += out_rows
    flat_ref[base : base + 1, :] = jnp.sum(d_raw, axis=0, keepdims=True)
    for m in range(members):
        for store in stores(m):
            store.wait()

    finish()
    for i in range(PH * PW // 8):
        for h in range(halves):
            flat_ref[pl.ds(8 * i * halves + h, 8, stride=halves), :] = end_grad[i * halves + h]


def finish_kernel(flat_size, flat_ref, summary_ref, sea_ref, vel_ref, flat_out, summary_out, sea_out, vel_out, held, load_sem, store_sem):
    members = sea_ref.shape[0]
    sources = [sea_ref.at[m] for m in range(members)] + [vel_ref.at[i, m] for i in (0, 1) for m in range(members)]
    targets = [sea_out.at[m] for m in range(members)] + [vel_out.at[i, m] for i in (0, 1) for m in range(members)]
    loads = [pltpu.make_async_copy(src, held.at[i], load_sem.at[i]) for i, src in enumerate(sources)]
    stores = [pltpu.make_async_copy(held.at[i], dst, store_sem.at[i]) for i, dst in enumerate(targets)]
    for load in loads:
        load.start()
    for load, store in zip(loads, stores):
        load.wait()
        store.start()
    flat = flat_ref[...]
    mean = jnp.sum(jnp.sum(flat * flat, axis=0, keepdims=True), axis=1, keepdims=True) / flat_size
    flat_out[...] = flat * (-1.0 / jnp.sqrt(mean + EPSILON))
    summary_out[...] = summary_ref[...]
    for store in stores:
        store.wait()


def shards(
    sea_surface, velocity, levels, wind_basis, proposals, member_ids, conv_weight,
    couple_in, couple_in_bias, couple_out, couple_out_bias,
):
    members, rows, cols = sea_surface.shape
    n_lon, n_lat, n_grp = lax.axis_size("lon"), lax.axis_size("lat"), lax.axis_size("grp")
    n_z = n_lon // 2
    n_plane = n_lat * n_grp
    n_wide = n_lon // n_z * n_plane
    n_items = members * STEPS
    per_dev = n_items // n_lon
    cells, feat = conv_weight.shape
    hid = couple_in.shape[1]
    height, width = rows + 16, cols + LANES
    weights = (couple_in, couple_in_bias, couple_out, couple_out_bias)
    flat_size = cells * feat + sum(w.size for w in weights)
    flat_rows = -(-flat_size // (8 * LANES)) * 8
    pieces = cells // 8 * (feat // LANES)
    per = pieces // n_wide
    shape = jax.ShapeDtypeStruct
    vmem, dma = pltpu.VMEM, pltpu.SemaphoreType.DMA
    summary, flat, sea, vel = pl.pallas_call(
        functools.partial(main_kernel, n_z),
        out_shape=(
            shape((per_dev, feat), F32),
            shape((flat_rows, LANES), F32),
            shape(sea_surface.shape, F32),
            shape(velocity.shape, F32),
        ),
        in_specs=[SMEM] * 2 + [VMEM] * 8 + [ANY] * 3,
        out_specs=(VMEM, VMEM, ANY, ANY),
        scratch_shapes=[
            vmem((members, 4, height, width), F32),
            vmem(wind_basis.shape, BF16),
            vmem((height, width), F32),
            vmem((height, width), F32),
            vmem((height, width), F32),
            vmem((height, width), F32),
            vmem((rows // PH * (cols // PW), cells), BF16),
            vmem((n_items, cells, feat), F32),
            vmem((rows, LANES), F32),
            vmem((rows, LANES), F32),
            vmem((2, 16, cols), jnp.int32),
            vmem((2, rows, LANES), F32),
            vmem((2, rows, LANES), jnp.int32),
            vmem((4, 8, LANES), F32),
            vmem((4, 16, LANES), jnp.int32),
            vmem((proposals.shape[0], LANES), F32),
            vmem((LANES, hid), F32),
            vmem((feat, hid), F32),
            vmem((LANES, hid), F32),
            vmem((1, LANES), F32),
            vmem((n_items, LANES), F32),
            vmem((n_items, feat), F32),
            vmem((n_lon, n_items, feat), F32),
            vmem((n_plane, n_items, feat), F32),
            vmem((n_items, feat), F32),
            vmem((pieces, 8, LANES), F32),
            vmem((n_wide, per, 8, LANES), F32),
            vmem((n_z, per, 8, LANES), F32),
            vmem((pieces, 8, LANES), F32),
            vmem((hid, LANES), F32),
            dma((4,)),
            dma((members, 3)),
            dma((members, 2)),
            dma((members, 2)),
            dma((14,)),
            dma((14,)),
            dma((members, n_lon)),
            dma((members, n_lon)),
            dma((members, n_plane)),
            dma((members, n_plane)),
            dma((3, n_wide)),
            dma((3, n_wide)),
        ],
        compiler_params=pltpu.CompilerParams(collective_id=0, has_side_effects=True),
        name="ensemble",
    )(
        member_ids, proposals, member_ids.reshape(1, -1), proposals, levels, conv_weight, couple_in,
        couple_in_bias.reshape(1, -1), couple_out.T, couple_out_bias.reshape(1, -1),
        sea_surface, velocity, wind_basis,
    )
    flat, summary, sea, vel = pl.pallas_call(
        functools.partial(finish_kernel, float(flat_size)),
        out_shape=(
            shape(flat.shape, F32), shape(summary.shape, F32), shape(sea.shape, F32), shape(vel.shape, F32),
        ),
        in_specs=[VMEM, VMEM, ANY, ANY],
        out_specs=(VMEM, VMEM, ANY, ANY),
        scratch_shapes=[
            vmem((3 * members, rows, cols), F32),
            dma((3 * members,)),
            dma((3 * members,)),
        ],
        name="finish",
    )(flat, summary, sea, vel)
    return sea, vel, summary.reshape((1, 1, 1) + summary.shape), flat.reshape(-1)[:flat_size]


def solution(mesh):
    in_specs = (
        P("grp", "lat", "lon"),
        P(None, "grp", "lat", "lon"),
        P("lat", "lon"),
        P(None, "lat", "lon"),
        P(), P(), P(), P(), P(), P(), P(),
    )
    out_specs = (
        P("grp", "lat", "lon"),
        P(None, "grp", "lat", "lon"),
        P("lon", "lat", "grp", None, None),
        P(),
    )
    return jax.shard_map(shards, mesh=mesh, in_specs=in_specs, out_specs=out_specs, check_vma=False)
```

```python
import functools
import math

import jax
import jax.numpy as jnp
from jax import lax
from jax.experimental import pallas as pl
from jax.experimental.pallas import tpu as pltpu
from jax.sharding import PartitionSpec as P

STEPS = 8
NLEV = 50
PH = 8
PW = 16
GRAVITY = 0.45
DRAG_RATE = 0.02
CORI_BASE = 0.05
CORI_SLOPE = 0.1
WIND_SCALE = 0.05
EPSILON = 1e-06
HALF = 8
LANES = 128
F32 = jnp.float32
BF16 = jnp.bfloat16
MESH = pl.DeviceIdType.MESH
ANY = pl.BlockSpec(memory_space=pl.ANY)
VMEM = pl.BlockSpec(memory_space=pltpu.VMEM)
SMEM = pl.BlockSpec(memory_space=pltpu.SMEM)


def iota(shape, dim):
    return lax.broadcasted_iota(jnp.int32, shape, dim)


def block_transposed(tile):
    block = iota((8, LANES), 1) // PW
    tile = pltpu.roll(tile, 0, 1, stride=PW, stride_axis=0)
    for bit in (1, 2, 4):
        tile = jnp.where((block & bit) != 0, pltpu.roll(tile, 8 - bit, 0), tile)
    return pltpu.roll(tile, 0, 1, stride=PW, stride_axis=0)


ROWS_OVER = (((0,), (0,)), ((), ()))
COLS_OVER = (((1,), (1,)), ((), ()))


def halves_of(x):
    high = x.astype(BF16)
    return high, (x - high.astype(F32)).astype(BF16)


def product(a, b, dims=(((1,), (0,)), ((), ()))):
    dot = functools.partial(lax.dot_general, dimension_numbers=dims, preferred_element_type=F32)
    total = dot(a[0], b[0])
    small = dot(a[0], b[1])
    if len(a) > 1:
        small = small + dot(a[1], b[0])
    return total + small


def flow_gradients(params, summ, w_low, w_sum, b_in, w_out, b_out):
    lane = iota(params.shape, 1)
    hidden = jnp.tanh(product(halves_of(params), w_low) + product(summ, w_sum) + b_in)
    raw = product(halves_of(hidden), w_out, COLS_OVER) + b_out
    log_scale = jnp.tanh(raw)
    scaled = pltpu.roll(params, LANES - HALF, 1) * jnp.exp(log_scale)
    latent = scaled + pltpu.roll(raw, LANES - HALF, 1)
    d_scale = (latent * scaled - 1.0) * (1.0 - log_scale * log_scale)
    d_raw = jnp.where(
        lane < HALF, d_scale, jnp.where(lane < 2 * HALF, pltpu.roll(latent, HALF, 1), 0.0)
    )
    d_hidden = product(halves_of(d_raw), w_out) * (1.0 - hidden * hidden)
    return hidden, d_raw, d_hidden


LEVEL, EAST, NORTH, FORCE = range(4)


def main_kernel(
    n_z, ids_s, prop_s, ids_ref, prop_ref, lev_ref, conv_ref, b_in_ref, w_out_ref, b_out_ref,
    sea_ref, vel_ref, wind_ref, w_in_ref,
    summary_ref, flat_ref, sea_out, vel_out,
    state, wind, w_in, hu_ref, hue_ref, hv_ref, hvu_ref, patches, gram, east_pack, west_pack, east_wind, west_wind,
    rowl_ref, colf_ref, colw_ref, corf_ref, corw_ref,
    prop_pad, w_low, w_sum, w_out_pad, b_out_pad, near_par, part, parts, all_sum, ds_ref,
    near_grad, got_grad, mid_grad, end_grad, out_pad,
    load_sem, store_sem, row_send, row_recv, edge_send, edge_recv, part_send, part_recv, sum_send, sum_recv,
    grad_send, grad_recv,
):
    members, _, height, width = state.shape
    rows, cols = height - 16, width - LANES
    n_lon, n_lat, n_grp = lax.axis_size("lon"), lax.axis_size("lat"), lax.axis_size("grp")
    lon, lat, grp = lax.axis_index("lon"), lax.axis_index("lat"), lax.axis_index("grp")
    total_rows, total_cols = rows * n_lat, cols * n_lon
    n_plane, n_hi = n_lat * n_grp, n_lon // n_z
    n_wide = n_hi * n_plane
    plane = lat * n_grp + grp
    hi, z = lon // n_z, lax.rem(lon, n_z)
    wide = hi * n_plane + plane
    n_members = prop_ref.shape[0]
    n_items = members * STEPS
    per_dev = n_items // n_lon
    feat = conv_ref.shape[1]
    hid = w_in_ref.shape[1]
    inv_root = 1.0 / math.sqrt(rows // PH * (total_cols // PW))
    own_rows, own_cols = slice(8, rows + 8), slice(0, cols)

    def lon_peer(d):
        to = lax.rem(lon + d, n_lon)
        return to, {"lon": to}

    def plane_peer(d):
        to = lax.rem(plane + d, n_plane)
        return to, {"lat": to // n_grp, "grp": lax.rem(to, n_grp)}

    def z_peer(d):
        to = lax.rem(z + d, n_z)
        return to, {"lon": hi * n_z + to}

    def wide_peer(d):
        to = lax.rem(wide + d, n_wide)
        rest = lax.rem(to, n_plane)
        return to, {"lon": (to // n_plane) * n_z + z, "lat": rest // n_grp, "grp": lax.rem(rest, n_grp)}

    east, west = lax.rem(lon + 1, n_lon), lax.rem(lon + n_lon - 1, n_lon)
    north, south = lax.rem(lat + 1, n_lat), lax.rem(lat + n_lat - 1, n_lat)

    barrier = pltpu.get_barrier_semaphore()
    for to_lat in (lat, north, south):
        for to_lon in (lon, east, west):
            if to_lat is lat and to_lon is lon:
                continue
            pl.semaphore_signal(
                barrier, inc=1, device_id={"lon": to_lon, "lat": to_lat}, device_id_type=MESH
            )

    def greet(peer):
        def body(d, carry):
            pl.semaphore_signal(barrier, inc=1, device_id=peer(d)[1], device_id_type=MESH)
            return carry

        return body

    lax.fori_loop(1, n_lon, greet(lon_peer), 0)
    lax.fori_loop(1, n_wide, greet(wide_peer), 0)

    loads = [
        pltpu.make_async_copy(sea_ref, state.at[:, LEVEL, own_rows, own_cols], load_sem.at[0]),
        pltpu.make_async_copy(vel_ref.at[0], state.at[:, EAST, own_rows, own_cols], load_sem.at[1]),
        pltpu.make_async_copy(vel_ref.at[1], state.at[:, NORTH, own_rows, own_cols], load_sem.at[2]),
        pltpu.make_async_copy(wind_ref, wind, load_sem.at[3]),
        pltpu.make_async_copy(w_in_ref, w_in, load_sem.at[4]),
    ]
    for load in loads:
        load.start()
    for load in loads[:3]:
        load.wait()

    slot = iota((rows, LANES), 1) // 8

    def pack(packed, fields):
        for s, (m, f) in enumerate(fields):
            right = state[m, f, own_rows, cols - LANES : cols]
            left = state[m, f, own_rows, :LANES]
            packed = tuple(
                jnp.where(slot == s, pltpu.roll(edge, shift, 1) if shift else edge, before)
                for edge, shift, before in (
                    (right, (8 * s + 8) % LANES, packed[0]), (left, 8 * s, packed[1]),
                )
            )
        return packed

    blank = jnp.zeros((rows, LANES), F32)
    for ref, value in zip(
        (east_pack, west_pack), pack((blank, blank), [(m, f) for m in range(members) for f in range(3)])
    ):
        ref[...] = value

    pl.semaphore_wait(barrier, 8 + n_lon - 1 + n_wide - 1)

    edges = []

    def send(src, dst, to_lat, to_lon):
        i = len(edges)
        copy = pltpu.make_async_remote_copy(
            src_ref=src, dst_ref=dst, send_sem=edge_send.at[i], recv_sem=edge_recv.at[i],
            device_id={"lon": to_lon, "lat": to_lat}, device_id_type=MESH,
        )
        copy.start()
        edges.append(copy)

    top_rows, bottom_rows = (slice(rows, rows + 8), slice(8, 16)), (slice(0, 8), slice(rows + 8, rows + 16))

    def row_copy(m, side):
        return pltpu.make_async_remote_copy(
            src_ref=state.at[m, LEVEL:FORCE, top_rows[side], own_cols],
            dst_ref=state.at[m, LEVEL:FORCE, bottom_rows[side], own_cols],
            send_sem=row_send.at[m, side], recv_sem=row_recv.at[m, side],
            device_id={"lat": (north, south)[side]}, device_id_type=MESH,
        )

    def send_columns(packs, columns, corners, depth):
        for side, to_lon in ((0, east), (1, west)):
            send(packs[side], columns.at[side], lat, to_lon)
        for side, to_lat, edge_rows in ((0, north, slice(rows - depth, rows)), (1, south, slice(0, depth))):
            for edge, to_lon in ((0, east), (1, west)):
                send(packs[edge].at[edge_rows], corners.at[2 * side + edge], to_lat, to_lon)

    send_columns((east_pack, west_pack), colf_ref, corf_ref, 8)
    for side, to_lat, wide_rows in ((0, north, slice(rows - 16, rows)), (1, south, slice(0, 16))):
        send(lev_ref.at[wide_rows], rowl_ref.at[side], to_lat, lon)
        row_copy(0, side).start()

    coeffs = []
    for m in range(members):
        row = ids_s[grp * members + m]
        for k in range(wind_ref.shape[0]):
            full = prop_s[row, k]
            scaled = full * 65537.0
            coeffs.append(scaled - (scaled - full))

    loads[3].wait()

    def force(r, carry):
        at = pl.ds(pl.multiple_of(r * 16, 16), 16)
        total = [None] * members
        for k in range(wind_ref.shape[0]):
            blow = wind[k, at, :].astype(F32)
            for m in range(members):
                term = coeffs[m * wind_ref.shape[0] + k] * blow
                total[m] = term if k == 0 else total[m] + term
        for m in range(members):
            state[m, FORCE, pl.ds(pl.multiple_of(r * 16 + 8, 8), 16), own_cols] = WIND_SCALE * total[m]
        return carry

    lax.fori_loop(0, rows // 16, force, 0)
    at_depth = (slot == members) | (slot == members + 1)
    depth_east = pltpu.roll(lev_ref[:, cols - LANES :].astype(F32), 8 * members + 2 * 8, 1)
    depth_west = pltpu.roll(lev_ref[:, :LANES].astype(F32), 8 * members, 1)
    for ref, value in zip(
        (east_wind, west_wind),
        pack(
            (jnp.where(at_depth, depth_east, 0.0), jnp.where(at_depth, depth_west, 0.0)),
            [(m, FORCE) for m in range(members)],
        ),
    ):
        ref[...] = value
    send_columns((east_wind, west_wind), colw_ref, corw_ref, 16)
    for side, to_lat in ((0, north), (1, south)):
        send(
            state.at[:, FORCE, top_rows[side], own_cols], state.at[:, FORCE, bottom_rows[side], own_cols],
            to_lat, lon,
        )
    for m in range(1, members):
        for side in (0, 1):
            row_copy(m, side).start()

    loads[4].wait()
    prop_pad[...] = jnp.zeros_like(prop_pad)
    prop_pad[:, : prop_ref.shape[1]] = prop_ref[...]

    def padded(x):
        return jnp.concatenate([x, jnp.zeros((LANES - x.shape[0], hid), F32)], axis=0)

    for ref, value in (
        (w_low, padded(w_in[:HALF])), (w_sum, w_in[HALF:]), (w_out_pad, padded(w_out_ref[...])),
    ):
        ref[0], ref[1] = halves_of(value)
    b_out_pad[...] = jnp.zeros_like(b_out_pad)
    b_out_pad[:, : 2 * HALF] = b_out_ref[...]
    b_in, b_out = b_in_ref[...], b_out_pad[...]
    pick = (iota((n_members, n_members), 0) == ids_ref[...]).astype(F32).astype(BF16)
    member_params = halves_of(product((pick,), halves_of(prop_pad[...]), ROWS_OVER))

    def params_of(n, group):
        chosen = group * members + lax.rem(n, n_items) // STEPS
        return product(((chosen == iota(n.shape, 1)).astype(F32).astype(BF16),), member_params)

    near_par[...] = params_of(iota((n_items, n_members), 0), grp)

    for copy in edges:
        copy.wait()

    inner_south, inner_north = lat > 0, lat < n_lat - 1
    low = iota((rows, LANES), 1) < 64
    low8 = iota((8, LANES), 1) < 64
    for m in range(members):
        for f in range(4):
            s, columns, corners = (m, colw_ref, corw_ref) if f == FORCE else (3 * m + f, colf_ref, corf_ref)

            def beyond(east_of, west_of, mask):
                return jnp.where(
                    mask, pltpu.roll(east_of, (LANES - 8 * s) % LANES, 1) if s else east_of,
                    pltpu.roll(west_of, (2 * LANES - 8 - 8 * s) % LANES, 1),
                )

            near_rows = slice(8, 16) if f == FORCE else slice(0, 8)
            state[m, f, own_rows, cols:] = beyond(columns[1], columns[0], low)
            state[m, f, 0:8, cols:] = beyond(corners[1, near_rows], corners[0, near_rows], low8)
            state[m, f, rows + 8 :, cols:] = beyond(corners[3, 0:8], corners[2, 0:8], low8)

    low16 = iota((16, LANES), 1) < 64

    def beside(east_of, west_of, mask):
        shift = LANES - 8 * members
        return jnp.where(mask, pltpu.roll(east_of, shift, 1), pltpu.roll(west_of, shift - 16, 1))

    below = jnp.concatenate([rowl_ref[0].astype(F32), beside(corw_ref[1], corw_ref[0], low16)], axis=1)
    above = jnp.concatenate([rowl_ref[1].astype(F32), beside(corw_ref[3], corw_ref[2], low16)], axis=1)
    own = jnp.concatenate([lev_ref[...].astype(F32), beside(colw_ref[1], colw_ref[0], low)], axis=1)
    depth = jnp.concatenate(
        [jnp.where(inner_south, below, 0.0), own, jnp.where(inner_north, above, 0.0)], axis=0
    ) / NLEV
    hu = 0.5 * (depth + pltpu.roll(depth, 1, 1))
    hv = 0.5 * (depth + pltpu.roll(depth, 1, 0))
    for ref, value in (
        (hu_ref, hu), (hue_ref, pltpu.roll(hu, width - 1, 1)),
        (hv_ref, hv), (hvu_ref, pltpu.roll(hv, rows + 31, 0)),
    ):
        ref[...] = value[8 : height + 8]

    sub = iota((8, width), 0)
    first, last = sub == 0, sub == 7
    keep_south = jnp.where(inner_south, 1.0, 0.0)
    keep_north = jnp.where(inner_north, 1.0, 0.0)
    n_tiles = height // 8

    def advance(m, step):
        n_cur = state[m, NORTH, 0:8, :]
        n_roll = pltpu.roll(n_cur, 7, 0)
        g_before = es_before = None
        held = []
        for k in range(n_tiles):
            at = slice(8 * k, 8 * k + 8)
            e = state[m, EAST, at, :]
            n = n_cur
            row = (lat * rows + (8 * k - 8) + iota((8, LANES), 0)).astype(F32)
            cu = 0.25 * (CORI_BASE + CORI_SLOPE * (row + 0.5) / total_rows)
            cv = 0.25 * (CORI_BASE + CORI_SLOPE * row / total_rows)
            cu = jnp.concatenate([cu] * (width // LANES), axis=1)
            cv = jnp.concatenate([cv] * (width // LANES), axis=1)
            if k + 1 < n_tiles:
                n_cur = state[m, NORTH, 8 * k + 8 : 8 * k + 16, :]
                n_next = pltpu.roll(n_cur, 7, 0)
                n_up = jnp.where(last, n_next, n_roll)
                n_roll = n_next
            else:
                n_up = n_roll
            e_e = pltpu.roll(e, width - 1, 1)
            new = state[m, LEVEL, at, :] - (
                (hue_ref[at, :] * e_e - hu_ref[at, :] * e) + (hvu_ref[at, :] * n_up - hv_ref[at, :] * n)
            )
            keep = {0: keep_south, n_tiles - 1: keep_north}.get(k)
            if keep is not None:
                new = new * keep
            g = GRAVITY * new
            g_w = pltpu.roll(g, 1, 1)
            g_roll = pltpu.roll(g, 1, 0)
            g_s = g_roll if k == 0 else jnp.where(first, g_before, g_roll)
            g_before = g_roll
            ns = n + n_up
            v_sum = ns + pltpu.roll(ns, 1, 1)
            es = e + e_e
            es_roll = pltpu.roll(es, 1, 0)
            u_sum = es + (es_roll if k == 0 else jnp.where(first, es_before, es_roll))
            es_before = es_roll
            e_new = (1.0 - DRAG_RATE) * e + (cu * v_sum - (g - g_w) + state[m, FORCE, at, :])
            n_new = (1.0 - DRAG_RATE) * n - (cv * u_sum + (g - g_s))
            if keep is not None:
                e_new = e_new * keep
                n_new = n_new * keep
            state[m, LEVEL, at, :] = new
            state[m, EAST, at, :] = e_new
            state[m, NORTH, at, :] = n_new
            if 0 < k < n_tiles - 1:
                held.append(
                    [block_transposed(new[:, c * LANES : (c + 1) * LANES]) for c in range(cols // LANES)]
                )
                if len(held) == 2:
                    for c in range(cols // LANES):
                        i = (k // 2 - 1) * (cols // LANES) + c
                        patches[16 * i : 16 * i + 16, :] = jnp.concatenate(
                            [held[0][c], held[1][c]], axis=0
                        ).astype(BF16)
                    held = []

        cells = patches[...]
        act = jnp.tanh(jnp.dot(cells, conv_ref[...], preferred_element_type=F32))
        item = m * STEPS + step
        part[pl.ds(item, 1), :] = jnp.sum(act, axis=0, keepdims=True) * inv_root
        high, rest = halves_of(1.0 - act * act)
        gram[item] = lax.dot_general(
            cells, high, ROWS_OVER, preferred_element_type=F32
        ) + lax.dot_general(cells, rest, ROWS_OVER, preferred_element_type=F32)

    def exchange(count, peer, source, target, sends, recvs):
        def copy(d):
            to, device = peer(d)
            return pltpu.make_async_remote_copy(
                src_ref=source(to), dst_ref=target(d), send_sem=sends.at[d],
                recv_sem=recvs.at[d], device_id=device, device_id_type=MESH,
            )

        def start(d, carry):
            copy(d).start()
            return carry

        def finish(d, carry):
            copy(d).wait()
            return carry

        return (
            lambda: lax.fori_loop(1, count, start, 0),
            lambda: lax.fori_loop(1, count, finish, 0),
        )

    def group(m):
        return pl.ds(pl.multiple_of(m * STEPS, STEPS), STEPS)

    def share_parts(m):
        return exchange(
            n_lon, lon_peer, lambda to: part.at[group(m)], lambda d: parts.at[lon, group(m)],
            part_send.at[m], part_recv.at[m],
        )

    def share_sums(m):
        return exchange(
            n_plane, plane_peer, lambda to: all_sum.at[plane, group(m)], lambda d: all_sum.at[plane, group(m)],
            sum_send.at[m], sum_recv.at[m],
        )

    def summarize(m):
        share_parts(m)[1]()
        total = parts[0, group(m), :]
        for other in range(1, n_lon):
            total = total + parts[other, group(m), :]
        all_sum[plane, group(m), :] = total
        share_sums(m)[0]()

    def stores(m):
        own = (own_rows, own_cols)
        return [
            pltpu.make_async_copy(state.at[(m, LEVEL) + own], sea_out.at[m], store_sem.at[m, 0]),
            pltpu.make_async_copy(state.at[(m, EAST) + own], vel_out.at[0, m], store_sem.at[m, 1]),
            pltpu.make_async_copy(state.at[(m, NORTH) + own], vel_out.at[1, m], store_sem.at[m, 2]),
        ]

    def member(m, carry):
        for side in (0, 1):
            row_copy(m, side).wait()

        @pl.when(lat == 0)
        def _():
            state[m, :, 0:8, :] = jnp.zeros((4, 8, width), F32)

        @pl.when(lat == n_lat - 1)
        def _():
            state[m, :, rows + 8 :, :] = jnp.zeros((4, 8, width), F32)

        def one(step, inner):
            advance(m, step)
            return inner

        lax.fori_loop(0, STEPS, one, 0)
        for store in stores(m):
            store.start()
        parts[lon, group(m), :] = part[group(m), :]
        share_parts(m)[0]()

        @pl.when(m > 0)
        def _():
            summarize(m - 1)

        return carry

    lax.fori_loop(0, members, member, 0)

    def slopes(first_row, end_row, total):
        at = slice(first_row, end_row)
        _, _, d_hidden = flow_gradients(
            near_par[at], halves_of(all_sum[plane, at, :]), w_low, w_sum, b_in, w_out_pad, b_out
        )
        ds_ref[at] = product(halves_of(d_hidden), w_sum, COLS_OVER) * inv_root
        return lax.fori_loop(
            first_row, end_row, lambda j, acc: acc + gram[j] * ds_ref[pl.ds(j, 1), :], total
        )

    final = (members - 1) * STEPS
    conv_grad = slopes(0, final, jnp.zeros(gram.shape[1:], F32))
    summarize(members - 1)
    conv_grad = slopes(final, n_items, conv_grad)
    halves = feat // LANES
    for i in range(PH * PW // 8):
        for h in range(halves):
            near_grad[i * halves + h] = conv_grad[8 * i : 8 * i + 8, h * LANES : (h + 1) * LANES]
    per = near_grad.shape[0] // n_wide
    start, finish = exchange(
        n_wide, wide_peer, lambda to: near_grad.at[pl.ds(to * per, per)], lambda d: got_grad.at[d],
        grad_send.at[0], grad_recv.at[0],
    )
    start()

    for q in range(per_dev):
        item = lon * per_dev + q
        summary_ref[q : q + 1, :] = all_sum[
            plane, pl.ds(lax.rem(item, members) * STEPS + item // members, 1), :
        ]

    for m in range(members):
        share_sums(m)[1]()
    n_all = iota((n_plane * n_items, n_members), 0)
    all_params = params_of(n_all, lax.rem(n_all // n_items, n_grp))
    summ = halves_of(all_sum[...].reshape(n_plane * n_items, feat))
    hidden, d_raw, d_hidden = flow_gradients(all_params, summ, w_low, w_sum, b_in, w_out_pad, b_out)

    got_grad[0] = near_grad[pl.ds(wide * per, per)]
    finish()
    total = got_grad[0]
    for d in range(1, n_wide):
        total = total + got_grad[d]
    mid_grad[z] = total
    start, finish = exchange(
        n_z, z_peer, lambda to: mid_grad.at[z], lambda d: mid_grad.at[z], grad_send.at[1], grad_recv.at[1]
    )
    start()

    conv_rows = PH * PW * feat // LANES
    w_cols = hid // LANES
    flat_ref[...] = jnp.zeros_like(flat_ref)
    d_halves = halves_of(d_hidden)
    g_low = product(halves_of(all_params), d_halves, ROWS_OVER)[:HALF]
    g_sum = product(summ, d_halves, ROWS_OVER)
    for h in range(w_cols):
        flat_ref[pl.ds(conv_rows + h, HALF, stride=w_cols), :] = g_low[:, h * LANES : (h + 1) * LANES]
        flat_ref[pl.ds(conv_rows + HALF * w_cols + h, feat, stride=w_cols), :] = g_sum[
            :, h * LANES : (h + 1) * LANES
        ]

    finish()
    total = mid_grad[0]
    for d in range(1, n_z):
        total = total + mid_grad[d]
    mine = pl.ds(wide * per, per)
    end_grad[mine] = total
    start, finish = exchange(
        n_wide, wide_peer, lambda to: end_grad.at[mine], lambda d: end_grad.at[mine],
        grad_send.at[2], grad_recv.at[2],
    )
    start()

    base = conv_rows + (HALF + feat) * w_cols
    g_b_in = jnp.sum(d_hidden, axis=0, keepdims=True)
    for h in range(w_cols):
        flat_ref[base + h : base + h + 1, :] = g_b_in[:, h * LANES : (h + 1) * LANES]
    base += w_cols
    out_pad[...] = product(halves_of(hidden), halves_of(d_raw), ROWS_OVER)
    per_row = LANES // (2 * HALF)
    out_rows = hid // per_row
    packed = out_pad[pl.ds(0, out_rows, stride=per_row), :]
    for s in range(1, per_row):
        packed = packed + pltpu.roll(
            out_pad[pl.ds(s, out_rows, stride=per_row), :], s * 2 * HALF, 1
        )
    flat_ref[base : base + out_rows, :] = packed
    base += out_rows
    flat_ref[base : base + 1, :] = jnp.sum(d_raw, axis=0, keepdims=True)
    for m in range(members):
        for store in stores(m):
            store.wait()

    finish()
    for i in range(PH * PW // 8):
        for h in range(halves):
            flat_ref[pl.ds(8 * i * halves + h, 8, stride=halves), :] = end_grad[i * halves + h]


def finish_kernel(flat_size, flat_ref, summary_ref, sea_ref, vel_ref, flat_out, summary_out, sea_out, vel_out, held, load_sem, store_sem):
    members = sea_ref.shape[0]
    sources = [sea_ref.at[m] for m in range(members)] + [vel_ref.at[i, m] for i in (0, 1) for m in range(members)]
    targets = [sea_out.at[m] for m in range(members)] + [vel_out.at[i, m] for i in (0, 1) for m in range(members)]
    loads = [pltpu.make_async_copy(src, held.at[i], load_sem.at[i]) for i, src in enumerate(sources)]
    stores = [pltpu.make_async_copy(held.at[i], dst, store_sem.at[i]) for i, dst in enumerate(targets)]
    for load in loads:
        load.start()
    for load, store in zip(loads, stores):
        load.wait()
        store.start()
    flat = flat_ref[...]
    mean = jnp.sum(jnp.sum(flat * flat, axis=0, keepdims=True), axis=1, keepdims=True) / flat_size
    flat_out[...] = flat * (-1.0 / jnp.sqrt(mean + EPSILON))
    summary_out[...] = summary_ref[...]
    for store in stores:
        store.wait()


def shards(
    sea_surface, velocity, levels, wind_basis, proposals, member_ids, conv_weight,
    couple_in, couple_in_bias, couple_out, couple_out_bias,
):
    members, rows, cols = sea_surface.shape
    n_lon, n_lat, n_grp = lax.axis_size("lon"), lax.axis_size("lat"), lax.axis_size("grp")
    n_z = n_lon // 2
    n_plane = n_lat * n_grp
    n_wide = n_lon // n_z * n_plane
    n_items = members * STEPS
    per_dev = n_items // n_lon
    cells, feat = conv_weight.shape
    hid = couple_in.shape[1]
    height, width = rows + 16, cols + LANES
    weights = (couple_in, couple_in_bias, couple_out, couple_out_bias)
    flat_size = cells * feat + sum(w.size for w in weights)
    flat_rows = -(-flat_size // (8 * LANES)) * 8
    pieces = cells // 8 * (feat // LANES)
    per = pieces // n_wide
    shape = jax.ShapeDtypeStruct
    vmem, dma = pltpu.VMEM, pltpu.SemaphoreType.DMA
    summary, flat, sea, vel = pl.pallas_call(
        functools.partial(main_kernel, n_z),
        out_shape=(
            shape((per_dev, feat), F32),
            shape((flat_rows, LANES), F32),
            shape(sea_surface.shape, F32),
            shape(velocity.shape, F32),
        ),
        in_specs=[SMEM] * 2 + [VMEM] * 7 + [ANY] * 4,
        out_specs=(VMEM, VMEM, ANY, ANY),
        scratch_shapes=[
            vmem((members, 4, height, width), F32),
            vmem(wind_basis.shape, BF16),
            vmem(couple_in.shape, F32),
            vmem((height, width), F32),
            vmem((height, width), F32),
            vmem((height, width), F32),
            vmem((height, width), F32),
            vmem((rows // PH * (cols // PW), cells), BF16),
            vmem((n_items, cells, feat), F32),
            vmem((rows, LANES), F32),
            vmem((rows, LANES), F32),
            vmem((rows, LANES), F32),
            vmem((rows, LANES), F32),
            vmem((2, 16, cols), jnp.int32),
            vmem((2, rows, LANES), F32),
            vmem((2, rows, LANES), F32),
            vmem((4, 8, LANES), F32),
            vmem((4, 16, LANES), F32),
            vmem((proposals.shape[0], LANES), F32),
            vmem((2, LANES, hid), BF16),
            vmem((2, feat, hid), BF16),
            vmem((2, LANES, hid), BF16),
            vmem((1, LANES), F32),
            vmem((n_items, LANES), F32),
            vmem((n_items, feat), F32),
            vmem((n_lon, n_items, feat), F32),
            vmem((n_plane, n_items, feat), F32),
            vmem((n_items, feat), F32),
            vmem((pieces, 8, LANES), F32),
            vmem((n_wide, per, 8, LANES), F32),
            vmem((n_z, per, 8, LANES), F32),
            vmem((pieces, 8, LANES), F32),
            vmem((hid, LANES), F32),
            dma((5,)),
            dma((members, 3)),
            dma((members, 2)),
            dma((members, 2)),
            dma((16,)),
            dma((16,)),
            dma((members, n_lon)),
            dma((members, n_lon)),
            dma((members, n_plane)),
            dma((members, n_plane)),
            dma((3, n_wide)),
            dma((3, n_wide)),
        ],
        compiler_params=pltpu.CompilerParams(collective_id=0, has_side_effects=True),
        name="ensemble",
    )(
        member_ids, proposals, member_ids.reshape(1, -1), proposals, levels, conv_weight,
        couple_in_bias.reshape(1, -1), couple_out.T, couple_out_bias.reshape(1, -1),
        sea_surface, velocity, wind_basis, couple_in,
    )
    flat, summary, sea, vel = pl.pallas_call(
        functools.partial(finish_kernel, float(flat_size)),
        out_shape=(
            shape(flat.shape, F32), shape(summary.shape, F32), shape(sea.shape, F32), shape(vel.shape, F32),
        ),
        in_specs=[VMEM, VMEM, ANY, ANY],
        out_specs=(VMEM, VMEM, ANY, ANY),
        scratch_shapes=[
            vmem((3 * members, rows, cols), F32),
            dma((3 * members,)),
            dma((3 * members,)),
        ],
        name="finish",
    )(flat, summary, sea, vel)
    return sea, vel, summary.reshape((1, 1, 1) + summary.shape), flat.reshape(-1)[:flat_size]


def solution(mesh):
    in_specs = (
        P("grp", "lat", "lon"),
        P(None, "grp", "lat", "lon"),
        P("lat", "lon"),
        P(None, "lat", "lon"),
        P(), P(), P(), P(), P(), P(), P(),
    )
    out_specs = (
        P("grp", "lat", "lon"),
        P(None, "grp", "lat", "lon"),
        P("lon", "lat", "grp", None, None),
        P(),
    )
    return jax.shard_map(shards, mesh=mesh, in_specs=in_specs, out_specs=out_specs, check_vma=False)
```

```python
import functools
import math

import jax
import jax.numpy as jnp
from jax import lax
from jax.experimental import pallas as pl
from jax.experimental.pallas import tpu as pltpu
from jax.sharding import PartitionSpec as P

STEPS = 8
NLEV = 50
PH = 8
PW = 16
GRAVITY = 0.45
DRAG_RATE = 0.02
CORI_BASE = 0.05
CORI_SLOPE = 0.1
WIND_SCALE = 0.05
EPSILON = 1e-06
HALF = 8
LANES = 128
F32 = jnp.float32
BF16 = jnp.bfloat16
MESH = pl.DeviceIdType.MESH
ANY = pl.BlockSpec(memory_space=pl.ANY)
VMEM = pl.BlockSpec(memory_space=pltpu.VMEM)
SMEM = pl.BlockSpec(memory_space=pltpu.SMEM)


def iota(shape, dim):
    return lax.broadcasted_iota(jnp.int32, shape, dim)


def block_transposed(tile):
    block = iota((8, LANES), 1) // PW
    tile = pltpu.roll(tile, 0, 1, stride=PW, stride_axis=0)
    for bit in (1, 2, 4):
        tile = jnp.where((block & bit) != 0, pltpu.roll(tile, 8 - bit, 0), tile)
    return pltpu.roll(tile, 0, 1, stride=PW, stride_axis=0)


ROWS_OVER = (((0,), (0,)), ((), ()))
COLS_OVER = (((1,), (1,)), ((), ()))


def halves_of(x):
    high = x.astype(BF16)
    return high, (x - high.astype(F32)).astype(BF16)


def product(a, b, dims=(((1,), (0,)), ((), ()))):
    dot = functools.partial(lax.dot_general, dimension_numbers=dims, preferred_element_type=F32)
    total = dot(a[0], b[0])
    small = dot(a[0], b[1])
    if len(a) > 1:
        small = small + dot(a[1], b[0])
    return total + small


def flow_gradients(params, summ, w_low, w_sum, b_in, w_out, b_out):
    lane = iota(params.shape, 1)
    hidden = jnp.tanh(product(halves_of(params), w_low) + product(summ, w_sum) + b_in)
    raw = product(halves_of(hidden), w_out, COLS_OVER) + b_out
    log_scale = jnp.tanh(raw)
    scaled = pltpu.roll(params, LANES - HALF, 1) * jnp.exp(log_scale)
    latent = scaled + pltpu.roll(raw, LANES - HALF, 1)
    d_scale = (latent * scaled - 1.0) * (1.0 - log_scale * log_scale)
    d_raw = jnp.where(
        lane < HALF, d_scale, jnp.where(lane < 2 * HALF, pltpu.roll(latent, HALF, 1), 0.0)
    )
    d_hidden = product(halves_of(d_raw), w_out) * (1.0 - hidden * hidden)
    return hidden, d_raw, d_hidden


LEVEL, EAST, NORTH, FORCE = range(4)
GROUP = 4


def main_kernel(
    n_z, ids_s, prop_s, ids_ref, prop_ref, lev_ref, conv_ref, b_in_ref, w_out_ref, b_out_ref,
    sea_ref, vel_ref, wind_ref, w_in_ref,
    summary_ref, flat_ref, sea_out, vel_out,
    state, wind, w_in, hu_ref, hue_ref, hv_ref, hvu_ref, patches, gram, east_pack, west_pack, east_wind, west_wind,
    rowl_ref, colf_ref, colw_ref, corf_ref, corw_ref,
    prop_pad, w_low, w_sum, w_out_pad, b_out_pad, near_par, part, parts, all_sum, ds_ref,
    near_grad, got_grad, mid_grad, end_grad, out_pad,
    load_sem, store_sem, row_send, row_recv, edge_send, edge_recv, part_send, part_recv, sum_send, sum_recv,
    grad_send, grad_recv,
):
    members, _, height, width = state.shape
    rows, cols = height - 16, width - LANES
    n_lon, n_lat, n_grp = lax.axis_size("lon"), lax.axis_size("lat"), lax.axis_size("grp")
    lon, lat, grp = lax.axis_index("lon"), lax.axis_index("lat"), lax.axis_index("grp")
    total_rows, total_cols = rows * n_lat, cols * n_lon
    n_plane, n_hi = n_lat * n_grp, n_lon // n_z
    n_wide = n_hi * n_plane
    plane = lat * n_grp + grp
    hi, z = lon // n_z, lax.rem(lon, n_z)
    wide = hi * n_plane + plane
    n_members = prop_ref.shape[0]
    n_items = members * STEPS
    per_dev = n_items // n_lon
    feat = conv_ref.shape[1]
    hid = w_in_ref.shape[1]
    inv_root = 1.0 / math.sqrt(rows // PH * (total_cols // PW))
    own_rows, own_cols = slice(8, rows + 8), slice(0, cols)

    def lon_peer(d):
        to = lax.rem(lon + d, n_lon)
        return to, {"lon": to}

    def plane_peer(d):
        to = lax.rem(plane + d, n_plane)
        return to, {"lat": to // n_grp, "grp": lax.rem(to, n_grp)}

    def z_peer(d):
        to = lax.rem(z + d, n_z)
        return to, {"lon": hi * n_z + to}

    def wide_peer(d):
        to = lax.rem(wide + d, n_wide)
        rest = lax.rem(to, n_plane)
        return to, {"lon": (to // n_plane) * n_z + z, "lat": rest // n_grp, "grp": lax.rem(rest, n_grp)}

    east, west = lax.rem(lon + 1, n_lon), lax.rem(lon + n_lon - 1, n_lon)
    north, south = lax.rem(lat + 1, n_lat), lax.rem(lat + n_lat - 1, n_lat)

    barrier = pltpu.get_barrier_semaphore()
    for to_lat in (lat, north, south):
        for to_lon in (lon, east, west):
            if to_lat is lat and to_lon is lon:
                continue
            pl.semaphore_signal(
                barrier, inc=1, device_id={"lon": to_lon, "lat": to_lat}, device_id_type=MESH
            )

    def greet(peer):
        def body(d, carry):
            pl.semaphore_signal(barrier, inc=1, device_id=peer(d)[1], device_id_type=MESH)
            return carry

        return body

    lax.fori_loop(1, n_lon, greet(lon_peer), 0)
    lax.fori_loop(1, n_wide, greet(wide_peer), 0)

    loads = [
        pltpu.make_async_copy(sea_ref, state.at[:, LEVEL, own_rows, own_cols], load_sem.at[0]),
        pltpu.make_async_copy(vel_ref.at[0], state.at[:, EAST, own_rows, own_cols], load_sem.at[1]),
        pltpu.make_async_copy(vel_ref.at[1], state.at[:, NORTH, own_rows, own_cols], load_sem.at[2]),
        pltpu.make_async_copy(wind_ref, wind, load_sem.at[3]),
        pltpu.make_async_copy(w_in_ref, w_in, load_sem.at[4]),
    ]
    for load in loads:
        load.start()
    for load in loads[:3]:
        load.wait()

    slot = iota((rows, LANES), 1) // 8

    def pack(packed, fields):
        for s, (m, f) in enumerate(fields):
            right = state[m, f, own_rows, cols - LANES : cols]
            left = state[m, f, own_rows, :LANES]
            packed = tuple(
                jnp.where(slot == s, pltpu.roll(edge, shift, 1) if shift else edge, before)
                for edge, shift, before in (
                    (right, (8 * s + 8) % LANES, packed[0]), (left, 8 * s, packed[1]),
                )
            )
        return packed

    blank = jnp.zeros((rows, LANES), F32)
    for ref, value in zip(
        (east_pack, west_pack), pack((blank, blank), [(m, f) for m in range(members) for f in range(3)])
    ):
        ref[...] = value

    pl.semaphore_wait(barrier, 8 + n_lon - 1 + n_wide - 1)

    edges = []

    def send(src, dst, to_lat, to_lon):
        i = len(edges)
        copy = pltpu.make_async_remote_copy(
            src_ref=src, dst_ref=dst, send_sem=edge_send.at[i], recv_sem=edge_recv.at[i],
            device_id={"lon": to_lon, "lat": to_lat}, device_id_type=MESH,
        )
        copy.start()
        edges.append(copy)

    top_rows, bottom_rows = (slice(rows, rows + 8), slice(8, 16)), (slice(0, 8), slice(rows + 8, rows + 16))

    def row_copy(m, side):
        return pltpu.make_async_remote_copy(
            src_ref=state.at[m, LEVEL:FORCE, top_rows[side], own_cols],
            dst_ref=state.at[m, LEVEL:FORCE, bottom_rows[side], own_cols],
            send_sem=row_send.at[m, side], recv_sem=row_recv.at[m, side],
            device_id={"lat": (north, south)[side]}, device_id_type=MESH,
        )

    def send_columns(packs, columns, corners, depth):
        for side, to_lon in ((0, east), (1, west)):
            send(packs[side], columns.at[side], lat, to_lon)
        for side, to_lat, edge_rows in ((0, north, slice(rows - depth, rows)), (1, south, slice(0, depth))):
            for edge, to_lon in ((0, east), (1, west)):
                send(packs[edge].at[edge_rows], corners.at[2 * side + edge], to_lat, to_lon)

    send_columns((east_pack, west_pack), colf_ref, corf_ref, 8)
    for side, to_lat, wide_rows in ((0, north, slice(rows - 16, rows)), (1, south, slice(0, 16))):
        send(lev_ref.at[wide_rows], rowl_ref.at[side], to_lat, lon)
        row_copy(0, side).start()

    coeffs = []
    for m in range(members):
        row = ids_s[grp * members + m]
        for k in range(wind_ref.shape[0]):
            full = prop_s[row, k]
            scaled = full * 65537.0
            coeffs.append(scaled - (scaled - full))

    loads[3].wait()

    def force(r, carry):
        at = pl.ds(pl.multiple_of(r * 16, 16), 16)
        total = [None] * members
        for k in range(wind_ref.shape[0]):
            blow = wind[k, at, :].astype(F32)
            for m in range(members):
                term = coeffs[m * wind_ref.shape[0] + k] * blow
                total[m] = term if k == 0 else total[m] + term
        for m in range(members):
            state[m, FORCE, pl.ds(pl.multiple_of(r * 16 + 8, 8), 16), own_cols] = WIND_SCALE * total[m]
        return carry

    lax.fori_loop(0, rows // 16, force, 0)
    at_depth = (slot == members) | (slot == members + 1)
    depth_east = pltpu.roll(lev_ref[:, cols - LANES :].astype(F32), 8 * members + 2 * 8, 1)
    depth_west = pltpu.roll(lev_ref[:, :LANES].astype(F32), 8 * members, 1)
    for ref, value in zip(
        (east_wind, west_wind),
        pack(
            (jnp.where(at_depth, depth_east, 0.0), jnp.where(at_depth, depth_west, 0.0)),
            [(m, FORCE) for m in range(members)],
        ),
    ):
        ref[...] = value
    send_columns((east_wind, west_wind), colw_ref, corw_ref, 16)
    for side, to_lat in ((0, north), (1, south)):
        send(
            state.at[:, FORCE, top_rows[side], own_cols], state.at[:, FORCE, bottom_rows[side], own_cols],
            to_lat, lon,
        )
    for m in range(1, members):
        for side in (0, 1):
            row_copy(m, side).start()

    loads[4].wait()
    prop_pad[...] = jnp.zeros_like(prop_pad)
    prop_pad[:, : prop_ref.shape[1]] = prop_ref[...]

    def padded(x):
        return jnp.concatenate([x, jnp.zeros((LANES - x.shape[0], hid), F32)], axis=0)

    for ref, value in (
        (w_low, padded(w_in[:HALF])), (w_sum, w_in[HALF:]), (w_out_pad, padded(w_out_ref[...])),
    ):
        ref[0], ref[1] = halves_of(value)
    b_out_pad[...] = jnp.zeros_like(b_out_pad)
    b_out_pad[:, : 2 * HALF] = b_out_ref[...]
    b_in, b_out = b_in_ref[...], b_out_pad[...]
    pick = (iota((n_members, n_members), 0) == ids_ref[...]).astype(F32).astype(BF16)
    member_params = halves_of(product((pick,), halves_of(prop_pad[...]), ROWS_OVER))

    def params_of(n, group):
        chosen = group * members + lax.rem(n, n_items) // STEPS
        return product(((chosen == iota(n.shape, 1)).astype(F32).astype(BF16),), member_params)

    near_par[...] = params_of(iota((n_items, n_members), 0), grp)

    for copy in edges:
        copy.wait()

    inner_south, inner_north = lat > 0, lat < n_lat - 1
    low = iota((rows, LANES), 1) < 64
    low8 = iota((8, LANES), 1) < 64
    for m in range(members):
        for f in range(4):
            s, columns, corners = (m, colw_ref, corw_ref) if f == FORCE else (3 * m + f, colf_ref, corf_ref)

            def beyond(east_of, west_of, mask):
                return jnp.where(
                    mask, pltpu.roll(east_of, (LANES - 8 * s) % LANES, 1) if s else east_of,
                    pltpu.roll(west_of, (2 * LANES - 8 - 8 * s) % LANES, 1),
                )

            near_rows = slice(8, 16) if f == FORCE else slice(0, 8)
            state[m, f, own_rows, cols:] = beyond(columns[1], columns[0], low)
            state[m, f, 0:8, cols:] = beyond(corners[1, near_rows], corners[0, near_rows], low8)
            state[m, f, rows + 8 :, cols:] = beyond(corners[3, 0:8], corners[2, 0:8], low8)

    low16 = iota((16, LANES), 1) < 64

    def beside(east_of, west_of, mask):
        shift = LANES - 8 * members
        return jnp.where(mask, pltpu.roll(east_of, shift, 1), pltpu.roll(west_of, shift - 16, 1))

    below = jnp.concatenate([rowl_ref[0].astype(F32), beside(corw_ref[1], corw_ref[0], low16)], axis=1)
    above = jnp.concatenate([rowl_ref[1].astype(F32), beside(corw_ref[3], corw_ref[2], low16)], axis=1)
    own = jnp.concatenate([lev_ref[...].astype(F32), beside(colw_ref[1], colw_ref[0], low)], axis=1)
    depth = jnp.concatenate(
        [jnp.where(inner_south, below, 0.0), own, jnp.where(inner_north, above, 0.0)], axis=0
    ) / NLEV
    hu = 0.5 * (depth + pltpu.roll(depth, 1, 1))
    hv = 0.5 * (depth + pltpu.roll(depth, 1, 0))
    for ref, value in (
        (hu_ref, hu), (hue_ref, pltpu.roll(hu, width - 1, 1)),
        (hv_ref, hv), (hvu_ref, pltpu.roll(hv, rows + 31, 0)),
    ):
        ref[...] = value[8 : height + 8]

    sub = iota((8, width), 0)
    first, last = sub == 0, sub == 7
    keep_south = jnp.where(inner_south, 1.0, 0.0)
    keep_north = jnp.where(inner_north, 1.0, 0.0)
    n_tiles = height // 8

    def advance(m, before):
        n_cur = state[m, NORTH, 0:8, :]
        n_roll = pltpu.roll(n_cur, 7, 0)
        g_before = es_before = None
        held = []
        for k in range(n_tiles):
            at = slice(8 * k, 8 * k + 8)
            e = state[m, EAST, at, :]
            n = n_cur
            row = (lat * rows + (8 * k - 8) + iota((8, LANES), 0)).astype(F32)
            cu = 0.25 * (CORI_BASE + CORI_SLOPE * (row + 0.5) / total_rows)
            cv = 0.25 * (CORI_BASE + CORI_SLOPE * row / total_rows)
            cu = jnp.concatenate([cu] * (width // LANES), axis=1)
            cv = jnp.concatenate([cv] * (width // LANES), axis=1)
            if k + 1 < n_tiles:
                n_cur = state[m, NORTH, 8 * k + 8 : 8 * k + 16, :]
                n_next = pltpu.roll(n_cur, 7, 0)
                n_up = jnp.where(last, n_next, n_roll)
                n_roll = n_next
            else:
                n_up = n_roll
            e_e = pltpu.roll(e, width - 1, 1)
            new = state[m, LEVEL, at, :] - (
                (hue_ref[at, :] * e_e - hu_ref[at, :] * e) + (hvu_ref[at, :] * n_up - hv_ref[at, :] * n)
            )
            keep = {0: keep_south, n_tiles - 1: keep_north}.get(k)
            if keep is not None:
                new = new * keep
            g = GRAVITY * new
            g_w = pltpu.roll(g, 1, 1)
            g_roll = pltpu.roll(g, 1, 0)
            g_s = g_roll if k == 0 else jnp.where(first, g_before, g_roll)
            g_before = g_roll
            ns = n + n_up
            v_sum = ns + pltpu.roll(ns, 1, 1)
            es = e + e_e
            es_roll = pltpu.roll(es, 1, 0)
            u_sum = es + (es_roll if k == 0 else jnp.where(first, es_before, es_roll))
            es_before = es_roll
            e_new = (1.0 - DRAG_RATE) * e + (cu * v_sum - (g - g_w) + state[m, FORCE, at, :])
            n_new = (1.0 - DRAG_RATE) * n - (cv * u_sum + (g - g_s))
            if keep is not None:
                e_new = e_new * keep
                n_new = n_new * keep
            state[m, LEVEL, at, :] = new
            state[m, EAST, at, :] = e_new
            state[m, NORTH, at, :] = n_new
            if 0 < k < n_tiles - 1:
                held.append(
                    [block_transposed(new[:, c * LANES : (c + 1) * LANES]) for c in range(cols // LANES)]
                )
                if len(held) == 2:
                    for c in range(cols // LANES):
                        i = (k // 2 - 1) * (cols // LANES) + c
                        patches[16 * i : 16 * i + 16, :] = jnp.concatenate(
                            [held[0][c], held[1][c]], axis=0
                        ).astype(BF16)
                    held = []

        item = before + 1
        cells = patches[...]
        act = jnp.tanh(jnp.dot(cells, conv_ref[...], preferred_element_type=F32))
        part[item // GROUP, pl.ds(lax.rem(item, GROUP), 1)] = jnp.sum(act, axis=0, keepdims=True) * inv_root
        high, rest = halves_of(1.0 - act * act)
        gram[item] = lax.dot_general(
            cells, high, ROWS_OVER, preferred_element_type=F32
        ) + lax.dot_general(cells, rest, ROWS_OVER, preferred_element_type=F32)

    def exchange(count, peer, source, target, sends, recvs, lead=1):
        def copy(d):
            to, device = peer(d)
            return pltpu.make_async_remote_copy(
                src_ref=source(to), dst_ref=target(d), send_sem=sends.at[d],
                recv_sem=recvs.at[d], device_id=device, device_id_type=MESH,
            )

        def start(d, carry):
            copy(1 + lax.rem(d + lead - 2, count - 1)).start()
            return carry

        def finish(d, carry):
            copy(1 + lax.rem(d + lead - 2, count - 1)).wait()
            return carry

        return (
            lambda: lax.fori_loop(1, count, start, 0),
            lambda: lax.fori_loop(1, count, finish, 0),
        )

    def group(m):
        return pl.ds(pl.multiple_of(m * STEPS, STEPS), STEPS)

    def share_parts(h):
        return exchange(
            n_lon, lon_peer, lambda to: part.at[h], lambda d: parts.at[lon, h],
            part_send.at[h], part_recv.at[h], 3 * n_lon // 4,
        )

    def share_sums(m):
        return exchange(
            n_plane, plane_peer, lambda to: all_sum.at[plane, group(m)], lambda d: all_sum.at[plane, group(m)],
            sum_send.at[m], sum_recv.at[m],
        )

    def summarize(h):
        share_parts(h)[1]()
        total = parts[0, h]
        for other in range(1, n_lon):
            total = total + parts[other, h]
        for r in range(GROUP):
            all_sum[plane, pl.ds(h * GROUP + r, 1), :] = total[r : r + 1]

        @pl.when(lax.rem(h, STEPS // GROUP) == STEPS // GROUP - 1)
        def _():
            share_sums(h // (STEPS // GROUP))[0]()

    def stores(m):
        own = (own_rows, own_cols)
        return [
            pltpu.make_async_copy(state.at[(m, LEVEL) + own], sea_out.at[m], store_sem.at[m, 0]),
            pltpu.make_async_copy(state.at[(m, EAST) + own], vel_out.at[0, m], store_sem.at[m, 1]),
            pltpu.make_async_copy(state.at[(m, NORTH) + own], vel_out.at[1, m], store_sem.at[m, 2]),
        ]

    n_groups = n_items // GROUP

    def part_done(h):
        parts[lon, h] = part[h]
        share_parts(h)[0]()

    def some_steps(h, carry):
        m = h // (STEPS // GROUP)

        @pl.when(lax.rem(h, STEPS // GROUP) == 0)
        def _():
            for side in (0, 1):
                row_copy(m, side).wait()

            @pl.when(lat == 0)
            def _():
                state[m, :, 0:8, :] = jnp.zeros((4, 8, width), F32)

            @pl.when(lat == n_lat - 1)
            def _():
                state[m, :, rows + 8 :, :] = jnp.zeros((4, 8, width), F32)

        def one(step, inner):
            item = h * GROUP + step
            advance(m, item - 1)
            return inner

        lax.fori_loop(0, GROUP, one, 0)

        @pl.when(lax.rem(h, STEPS // GROUP) == STEPS // GROUP - 1)
        def _():
            for store in stores(m):
                store.start()
        part_done(h)

        @pl.when(h > 0)
        def _():
            summarize(h - 1)

        return carry

    lax.fori_loop(0, n_groups, some_steps, 0)
    def slopes(first_row, end_row, total):
        at = slice(first_row, end_row)
        _, _, d_hidden = flow_gradients(
            near_par[at], halves_of(all_sum[plane, at, :]), w_low, w_sum, b_in, w_out_pad, b_out
        )
        ds_ref[at] = product(halves_of(d_hidden), w_sum, COLS_OVER) * inv_root
        return lax.fori_loop(
            first_row, end_row, lambda j, acc: acc + gram[j] * ds_ref[pl.ds(j, 1), :], total
        )

    final = n_items - 8
    conv_grad = slopes(0, final, jnp.zeros(gram.shape[1:], F32))
    summarize(n_groups - 1)
    conv_grad = slopes(final, n_items, conv_grad)
    halves = feat // LANES
    for i in range(PH * PW // 8):
        for h in range(halves):
            near_grad[i * halves + h] = conv_grad[8 * i : 8 * i + 8, h * LANES : (h + 1) * LANES]
    per = near_grad.shape[0] // n_wide
    start, finish = exchange(
        n_wide, wide_peer, lambda to: near_grad.at[pl.ds(to * per, per)], lambda d: got_grad.at[d],
        grad_send.at[0], grad_recv.at[0], 3 * n_wide // 4,
    )
    start()

    for q in range(per_dev):
        item = lon * per_dev + q
        summary_ref[q : q + 1, :] = all_sum[
            plane, pl.ds(lax.rem(item, members) * STEPS + item // members, 1), :
        ]

    for m in range(members):
        share_sums(m)[1]()
    n_all = iota((n_plane * n_items, n_members), 0)
    all_params = params_of(n_all, lax.rem(n_all // n_items, n_grp))
    summ = halves_of(all_sum[...].reshape(n_plane * n_items, feat))
    hidden, d_raw, d_hidden = flow_gradients(all_params, summ, w_low, w_sum, b_in, w_out_pad, b_out)

    got_grad[0] = near_grad[pl.ds(wide * per, per)]
    finish()
    total = got_grad[0]
    for d in range(1, n_wide):
        total = total + got_grad[d]
    mid_grad[z] = total
    start, finish = exchange(
        n_z, z_peer, lambda to: mid_grad.at[z], lambda d: mid_grad.at[z], grad_send.at[1], grad_recv.at[1]
    )
    start()

    conv_rows = PH * PW * feat // LANES
    w_cols = hid // LANES
    flat_ref[...] = jnp.zeros_like(flat_ref)
    d_halves = halves_of(d_hidden)
    g_low = product(halves_of(all_params), d_halves, ROWS_OVER)[:HALF]
    g_sum = product(summ, d_halves, ROWS_OVER)
    for h in range(w_cols):
        flat_ref[pl.ds(conv_rows + h, HALF, stride=w_cols), :] = g_low[:, h * LANES : (h + 1) * LANES]
        flat_ref[pl.ds(conv_rows + HALF * w_cols + h, feat, stride=w_cols), :] = g_sum[
            :, h * LANES : (h + 1) * LANES
        ]

    finish()
    total = mid_grad[0]
    for d in range(1, n_z):
        total = total + mid_grad[d]
    mine = pl.ds(wide * per, per)
    end_grad[mine] = total
    start, finish = exchange(
        n_wide, wide_peer, lambda to: end_grad.at[mine], lambda d: end_grad.at[mine],
        grad_send.at[2], grad_recv.at[2], 3 * n_wide // 4,
    )
    start()

    base = conv_rows + (HALF + feat) * w_cols
    g_b_in = jnp.sum(d_hidden, axis=0, keepdims=True)
    for h in range(w_cols):
        flat_ref[base + h : base + h + 1, :] = g_b_in[:, h * LANES : (h + 1) * LANES]
    base += w_cols
    out_pad[...] = product(halves_of(hidden), halves_of(d_raw), ROWS_OVER)
    per_row = LANES // (2 * HALF)
    out_rows = hid // per_row
    packed = out_pad[pl.ds(0, out_rows, stride=per_row), :]
    for s in range(1, per_row):
        packed = packed + pltpu.roll(
            out_pad[pl.ds(s, out_rows, stride=per_row), :], s * 2 * HALF, 1
        )
    flat_ref[base : base + out_rows, :] = packed
    base += out_rows
    flat_ref[base : base + 1, :] = jnp.sum(d_raw, axis=0, keepdims=True)
    for m in range(members):
        for store in stores(m):
            store.wait()

    finish()
    for i in range(PH * PW // 8):
        for h in range(halves):
            flat_ref[pl.ds(8 * i * halves + h, 8, stride=halves), :] = end_grad[i * halves + h]


def finish_kernel(
    flat_size, flat_ref, summary_ref, sea_ref, vel_ref, flat_out, summary_out, sea_out, vel_out,
    flat, summary, held, load_sem, store_sem,
):
    members = sea_ref.shape[0]
    moves = [(flat_ref, flat, flat_out), (summary_ref, summary, summary_out)]
    moves += [(sea_ref.at[m], held.at[m], sea_out.at[m]) for m in range(members)]
    moves += [
        (vel_ref.at[i, m], held.at[members * (i + 1) + m], vel_out.at[i, m])
        for i in (0, 1) for m in range(members)
    ]
    loads = [pltpu.make_async_copy(a, b, load_sem.at[i]) for i, (a, b, _) in enumerate(moves)]
    stores = [pltpu.make_async_copy(b, c, store_sem.at[i]) for i, (_, b, c) in enumerate(moves)]
    for load in loads:
        load.start()
    loads[0].wait()
    total = flat[...]
    mean = jnp.sum(jnp.sum(total * total, axis=0, keepdims=True), axis=1, keepdims=True) / flat_size
    flat[...] = total * (-1.0 / jnp.sqrt(mean + EPSILON))
    stores[0].start()
    for load, store in zip(loads[1:], stores[1:]):
        load.wait()
        store.start()
    for store in stores:
        store.wait()


def shards(
    sea_surface, velocity, levels, wind_basis, proposals, member_ids, conv_weight,
    couple_in, couple_in_bias, couple_out, couple_out_bias,
):
    members, rows, cols = sea_surface.shape
    n_lon, n_lat, n_grp = lax.axis_size("lon"), lax.axis_size("lat"), lax.axis_size("grp")
    n_z = n_lon // 2
    n_plane = n_lat * n_grp
    n_wide = n_lon // n_z * n_plane
    n_items = members * STEPS
    per_dev = n_items // n_lon
    cells, feat = conv_weight.shape
    hid = couple_in.shape[1]
    height, width = rows + 16, cols + LANES
    weights = (couple_in, couple_in_bias, couple_out, couple_out_bias)
    flat_size = cells * feat + sum(w.size for w in weights)
    flat_rows = -(-flat_size // (8 * LANES)) * 8
    pieces = cells // 8 * (feat // LANES)
    per = pieces // n_wide
    shape = jax.ShapeDtypeStruct
    vmem, dma = pltpu.VMEM, pltpu.SemaphoreType.DMA
    summary, flat, sea, vel = pl.pallas_call(
        functools.partial(main_kernel, n_z),
        out_shape=(
            shape((per_dev, feat), F32),
            shape((flat_rows, LANES), F32),
            shape(sea_surface.shape, F32),
            shape(velocity.shape, F32),
        ),
        in_specs=[SMEM] * 2 + [VMEM] * 7 + [ANY] * 4,
        out_specs=(VMEM, VMEM, ANY, ANY),
        scratch_shapes=[
            vmem((members, 4, height, width), F32),
            vmem(wind_basis.shape, BF16),
            vmem(couple_in.shape, F32),
            vmem((height, width), F32),
            vmem((height, width), F32),
            vmem((height, width), F32),
            vmem((height, width), F32),
            vmem((rows // PH * (cols // PW), cells), BF16),
            vmem((n_items + 1, cells, feat), F32),
            vmem((rows, LANES), F32),
            vmem((rows, LANES), F32),
            vmem((rows, LANES), F32),
            vmem((rows, LANES), F32),
            vmem((2, 16, cols), jnp.int32),
            vmem((2, rows, LANES), F32),
            vmem((2, rows, LANES), F32),
            vmem((4, 8, LANES), F32),
            vmem((4, 16, LANES), F32),
            vmem((proposals.shape[0], LANES), F32),
            vmem((2, LANES, hid), BF16),
            vmem((2, feat, hid), BF16),
            vmem((2, LANES, hid), BF16),
            vmem((1, LANES), F32),
            vmem((n_items, LANES), F32),
            vmem((n_items // GROUP + 1, GROUP, feat), F32),
            vmem((n_lon, n_items // GROUP, GROUP, feat), F32),
            vmem((n_plane, n_items, feat), F32),
            vmem((n_items, feat), F32),
            vmem((pieces, 8, LANES), F32),
            vmem((n_wide, per, 8, LANES), F32),
            vmem((n_z, per, 8, LANES), F32),
            vmem((pieces, 8, LANES), F32),
            vmem((hid, LANES), F32),
            dma((5,)),
            dma((members, 3)),
            dma((members, 2)),
            dma((members, 2)),
            dma((16,)),
            dma((16,)),
            dma((n_items // GROUP, n_lon)),
            dma((n_items // GROUP, n_lon)),
            dma((members, n_plane)),
            dma((members, n_plane)),
            dma((3, n_wide)),
            dma((3, n_wide)),
        ],
        compiler_params=pltpu.CompilerParams(collective_id=0, has_side_effects=True),
        name="ensemble",
    )(
        member_ids, proposals, member_ids.reshape(1, -1), proposals, levels, conv_weight,
        couple_in_bias.reshape(1, -1), couple_out.T, couple_out_bias.reshape(1, -1),
        sea_surface, velocity, wind_basis, couple_in,
    )
    flat, summary, sea, vel = pl.pallas_call(
        functools.partial(finish_kernel, float(flat_size)),
        out_shape=(
            shape(flat.shape, F32), shape(summary.shape, F32), shape(sea.shape, F32), shape(vel.shape, F32),
        ),
        in_specs=[ANY] * 4,
        out_specs=(ANY,) * 4,
        scratch_shapes=[
            vmem(flat.shape, F32),
            vmem(summary.shape, F32),
            vmem((3 * members, rows, cols), F32),
            dma((3 * members + 2,)),
            dma((3 * members + 2,)),
        ],
        name="finish",
    )(flat, summary, sea, vel)
    return sea, vel, summary.reshape((1, 1, 1) + summary.shape), flat.reshape(-1)[:flat_size]


def solution(mesh):
    in_specs = (
        P("grp", "lat", "lon"),
        P(None, "grp", "lat", "lon"),
        P("lat", "lon"),
        P(None, "lat", "lon"),
        P(), P(), P(), P(), P(), P(), P(),
    )
    out_specs = (
        P("grp", "lat", "lon"),
        P(None, "grp", "lat", "lon"),
        P("lon", "lat", "grp", None, None),
        P(),
    )
    return jax.shard_map(shards, mesh=mesh, in_specs=in_specs, out_specs=out_specs, check_vma=False)
```

```python
import functools
import math

import jax
import jax.numpy as jnp
from jax import lax
from jax.experimental import pallas as pl
from jax.experimental.pallas import tpu as pltpu
from jax.sharding import PartitionSpec as P

STEPS = 8
NLEV = 50
PH = 8
PW = 16
GRAVITY = 0.45
DRAG_RATE = 0.02
CORI_BASE = 0.05
CORI_SLOPE = 0.1
WIND_SCALE = 0.05
EPSILON = 1e-06
HALF = 8
LANES = 128
F32 = jnp.float32
BF16 = jnp.bfloat16
MESH = pl.DeviceIdType.MESH
ANY = pl.BlockSpec(memory_space=pl.ANY)
VMEM = pl.BlockSpec(memory_space=pltpu.VMEM)
SMEM = pl.BlockSpec(memory_space=pltpu.SMEM)


def iota(shape, dim):
    return lax.broadcasted_iota(jnp.int32, shape, dim)


def block_transposed(tile):
    block = iota((8, LANES), 1) // PW
    tile = pltpu.roll(tile, 0, 1, stride=PW, stride_axis=0)
    for bit in (1, 2, 4):
        tile = jnp.where((block & bit) != 0, pltpu.roll(tile, 8 - bit, 0), tile)
    return pltpu.roll(tile, 0, 1, stride=PW, stride_axis=0)


ROWS_OVER = (((0,), (0,)), ((), ()))
COLS_OVER = (((1,), (1,)), ((), ()))


def halves_of(x):
    high = x.astype(BF16)
    return high, (x - high.astype(F32)).astype(BF16)


def product(a, b, dims=(((1,), (0,)), ((), ()))):
    dot = functools.partial(lax.dot_general, dimension_numbers=dims, preferred_element_type=F32)
    total = dot(a[0], b[0])
    small = dot(a[0], b[1])
    if len(a) > 1:
        small = small + dot(a[1], b[0])
    return total + small


def flow_gradients(params, summ, w_low, w_sum, b_in, w_out, b_out):
    lane = iota(params.shape, 1)
    hidden = jnp.tanh(product(halves_of(params), w_low) + product(summ, w_sum) + b_in)
    raw = product(halves_of(hidden), w_out, COLS_OVER) + b_out
    log_scale = jnp.tanh(raw)
    scaled = pltpu.roll(params, LANES - HALF, 1) * jnp.exp(log_scale)
    latent = scaled + pltpu.roll(raw, LANES - HALF, 1)
    d_scale = (latent * scaled - 1.0) * (1.0 - log_scale * log_scale)
    d_raw = jnp.where(
        lane < HALF, d_scale, jnp.where(lane < 2 * HALF, pltpu.roll(latent, HALF, 1), 0.0)
    )
    d_hidden = product(halves_of(d_raw), w_out) * (1.0 - hidden * hidden)
    return hidden, d_raw, d_hidden


LEVEL, EAST, NORTH, FORCE = range(4)
GROUP = 8
LAG = 1


def main_kernel(
    n_z, ids_s, prop_s, ids_ref, prop_ref, lev_ref, conv_ref, b_in_ref, w_out_ref, b_out_ref,
    sea_ref, vel_ref, wind_ref, w_in_ref,
    summary_ref, flat_ref, sea_out, vel_out,
    state, wind, w_in, hu_ref, hue_ref, hv_ref, hvu_ref, patches, gram, east_pack, west_pack, east_wind, west_wind,
    rowl_ref, colf_ref, colw_ref, corf_ref, corw_ref,
    prop_pad, w_low, w_sum, w_out_pad, b_out_pad, near_par, part, parts, all_sum, ds_ref,
    near_grad, got_grad, mid_grad, end_grad, out_pad,
    load_sem, store_sem, row_send, row_recv, edge_send, edge_recv, part_send, part_recv, sum_send, sum_recv,
    grad_send, grad_recv,
):
    members, _, height, width = state.shape
    rows, cols = height - 16, width - LANES
    n_lon, n_lat, n_grp = lax.axis_size("lon"), lax.axis_size("lat"), lax.axis_size("grp")
    lon, lat, grp = lax.axis_index("lon"), lax.axis_index("lat"), lax.axis_index("grp")
    total_rows, total_cols = rows * n_lat, cols * n_lon
    n_plane, n_hi = n_lat * n_grp, n_lon // n_z
    n_wide = n_hi * n_plane
    plane = lat * n_grp + grp
    hi, z = lon // n_z, lax.rem(lon, n_z)
    wide = hi * n_plane + plane
    n_members = prop_ref.shape[0]
    n_items = members * STEPS
    per_dev = n_items // n_lon
    feat = conv_ref.shape[1]
    hid = w_in_ref.shape[1]
    inv_root = 1.0 / math.sqrt(rows // PH * (total_cols // PW))
    own_rows, own_cols = slice(8, rows + 8), slice(0, cols)

    def lon_peer(d):
        to = lax.rem(lon + d, n_lon)
        return to, {"lon": to}

    def plane_peer(d):
        to = lax.rem(plane + d, n_plane)
        return to, {"lat": to // n_grp, "grp": lax.rem(to, n_grp)}

    def z_peer(d):
        to = lax.rem(z + d, n_z)
        return to, {"lon": hi * n_z + to}

    def wide_peer(d):
        to = lax.rem(wide + d, n_wide)
        rest = lax.rem(to, n_plane)
        return to, {"lon": (to // n_plane) * n_z + z, "lat": rest // n_grp, "grp": lax.rem(rest, n_grp)}

    east, west = lax.rem(lon + 1, n_lon), lax.rem(lon + n_lon - 1, n_lon)
    north, south = lax.rem(lat + 1, n_lat), lax.rem(lat + n_lat - 1, n_lat)

    barrier = pltpu.get_barrier_semaphore()
    for to_lat in (lat, north, south):
        for to_lon in (lon, east, west):
            if to_lat is lat and to_lon is lon:
                continue
            pl.semaphore_signal(
                barrier, inc=1, device_id={"lon": to_lon, "lat": to_lat}, device_id_type=MESH
            )

    def greet(peer):
        def body(d, carry):
            pl.semaphore_signal(barrier, inc=1, device_id=peer(d)[1], device_id_type=MESH)
            return carry

        return body

    lax.fori_loop(1, n_lon, greet(lon_peer), 0)
    lax.fori_loop(1, n_wide, greet(wide_peer), 0)

    loads = [
        pltpu.make_async_copy(sea_ref, state.at[:, LEVEL, own_rows, own_cols], load_sem.at[0]),
        pltpu.make_async_copy(vel_ref.at[0], state.at[:, EAST, own_rows, own_cols], load_sem.at[1]),
        pltpu.make_async_copy(vel_ref.at[1], state.at[:, NORTH, own_rows, own_cols], load_sem.at[2]),
        pltpu.make_async_copy(wind_ref, wind, load_sem.at[3]),
        pltpu.make_async_copy(w_in_ref, w_in, load_sem.at[4]),
    ]
    for load in loads:
        load.start()
    for load in loads[:3]:
        load.wait()

    slot = iota((rows, LANES), 1) // 8

    def pack(packed, fields):
        for s, (m, f) in enumerate(fields):
            right = state[m, f, own_rows, cols - LANES : cols]
            left = state[m, f, own_rows, :LANES]
            packed = tuple(
                jnp.where(slot == s, pltpu.roll(edge, shift, 1) if shift else edge, before)
                for edge, shift, before in (
                    (right, (8 * s + 8) % LANES, packed[0]), (left, 8 * s, packed[1]),
                )
            )
        return packed

    blank = jnp.zeros((rows, LANES), F32)
    for ref, value in zip(
        (east_pack, west_pack), pack((blank, blank), [(m, f) for m in range(members) for f in range(3)])
    ):
        ref[...] = value

    pl.semaphore_wait(barrier, 8 + n_lon - 1 + n_wide - 1)

    edges = []

    def send(src, dst, to_lat, to_lon):
        i = len(edges)
        copy = pltpu.make_async_remote_copy(
            src_ref=src, dst_ref=dst, send_sem=edge_send.at[i], recv_sem=edge_recv.at[i],
            device_id={"lon": to_lon, "lat": to_lat}, device_id_type=MESH,
        )
        copy.start()
        edges.append(copy)

    top_rows, bottom_rows = (slice(rows, rows + 8), slice(8, 16)), (slice(0, 8), slice(rows + 8, rows + 16))

    def row_copy(m, side):
        return pltpu.make_async_remote_copy(
            src_ref=state.at[m, LEVEL:FORCE, top_rows[side], own_cols],
            dst_ref=state.at[m, LEVEL:FORCE, bottom_rows[side], own_cols],
            send_sem=row_send.at[m, side], recv_sem=row_recv.at[m, side],
            device_id={"lat": (north, south)[side]}, device_id_type=MESH,
        )

    def send_columns(packs, columns, corners, depth):
        for side, to_lon in ((0, east), (1, west)):
            send(packs[side], columns.at[side], lat, to_lon)
        for side, to_lat, edge_rows in ((0, north, slice(rows - depth, rows)), (1, south, slice(0, depth))):
            for edge, to_lon in ((0, east), (1, west)):
                send(packs[edge].at[edge_rows], corners.at[2 * side + edge], to_lat, to_lon)

    send_columns((east_pack, west_pack), colf_ref, corf_ref, 8)
    for side, to_lat, wide_rows in ((0, north, slice(rows - 16, rows)), (1, south, slice(0, 16))):
        send(lev_ref.at[wide_rows], rowl_ref.at[side], to_lat, lon)
        row_copy(0, side).start()

    coeffs = []
    for m in range(members):
        row = ids_s[grp * members + m]
        for k in range(wind_ref.shape[0]):
            full = prop_s[row, k]
            scaled = full * 65537.0
            coeffs.append(scaled - (scaled - full))

    loads[3].wait()

    def force(r, carry):
        at = pl.ds(pl.multiple_of(r * 16, 16), 16)
        total = [None] * members
        for k in range(wind_ref.shape[0]):
            blow = wind[k, at, :].astype(F32)
            for m in range(members):
                term = coeffs[m * wind_ref.shape[0] + k] * blow
                total[m] = term if k == 0 else total[m] + term
        for m in range(members):
            state[m, FORCE, pl.ds(pl.multiple_of(r * 16 + 8, 8), 16), own_cols] = WIND_SCALE * total[m]
        return carry

    lax.fori_loop(0, rows // 16, force, 0)
    at_depth = (slot == members) | (slot == members + 1)
    depth_east = pltpu.roll(lev_ref[:, cols - LANES :].astype(F32), 8 * members + 2 * 8, 1)
    depth_west = pltpu.roll(lev_ref[:, :LANES].astype(F32), 8 * members, 1)
    for ref, value in zip(
        (east_wind, west_wind),
        pack(
            (jnp.where(at_depth, depth_east, 0.0), jnp.where(at_depth, depth_west, 0.0)),
            [(m, FORCE) for m in range(members)],
        ),
    ):
        ref[...] = value
    send_columns((east_wind, west_wind), colw_ref, corw_ref, 16)
    for side, to_lat in ((0, north), (1, south)):
        send(
            state.at[:, FORCE, top_rows[side], own_cols], state.at[:, FORCE, bottom_rows[side], own_cols],
            to_lat, lon,
        )
    for m in range(1, members):
        for side in (0, 1):
            row_copy(m, side).start()

    loads[4].wait()
    prop_pad[...] = jnp.zeros_like(prop_pad)
    prop_pad[:, : prop_ref.shape[1]] = prop_ref[...]

    def padded(x):
        return jnp.concatenate([x, jnp.zeros((LANES - x.shape[0], hid), F32)], axis=0)

    for ref, value in (
        (w_low, padded(w_in[:HALF])), (w_sum, w_in[HALF:]), (w_out_pad, padded(w_out_ref[...])),
    ):
        ref[0], ref[1] = halves_of(value)
    b_out_pad[...] = jnp.zeros_like(b_out_pad)
    b_out_pad[:, : 2 * HALF] = b_out_ref[...]
    b_in, b_out = b_in_ref[...], b_out_pad[...]
    pick = (iota((n_members, n_members), 0) == ids_ref[...]).astype(F32).astype(BF16)
    member_params = halves_of(product((pick,), halves_of(prop_pad[...]), ROWS_OVER))

    def params_of(n, group):
        chosen = group * members + lax.rem(n, n_items) // STEPS
        return product(((chosen == iota(n.shape, 1)).astype(F32).astype(BF16),), member_params)

    near_par[...] = params_of(iota((n_items, n_members), 0), grp)

    for copy in edges:
        copy.wait()

    inner_south, inner_north = lat > 0, lat < n_lat - 1
    low = iota((rows, LANES), 1) < 64
    low8 = iota((8, LANES), 1) < 64
    for m in range(members):
        for f in range(4):
            s, columns, corners = (m, colw_ref, corw_ref) if f == FORCE else (3 * m + f, colf_ref, corf_ref)

            def beyond(east_of, west_of, mask):
                return jnp.where(
                    mask, pltpu.roll(east_of, (LANES - 8 * s) % LANES, 1) if s else east_of,
                    pltpu.roll(west_of, (2 * LANES - 8 - 8 * s) % LANES, 1),
                )

            near_rows = slice(8, 16) if f == FORCE else slice(0, 8)
            state[m, f, own_rows, cols:] = beyond(columns[1], columns[0], low)
            state[m, f, 0:8, cols:] = beyond(corners[1, near_rows], corners[0, near_rows], low8)
            state[m, f, rows + 8 :, cols:] = beyond(corners[3, 0:8], corners[2, 0:8], low8)

    low16 = iota((16, LANES), 1) < 64

    def beside(east_of, west_of, mask):
        shift = LANES - 8 * members
        return jnp.where(mask, pltpu.roll(east_of, shift, 1), pltpu.roll(west_of, shift - 16, 1))

    below = jnp.concatenate([rowl_ref[0].astype(F32), beside(corw_ref[1], corw_ref[0], low16)], axis=1)
    above = jnp.concatenate([rowl_ref[1].astype(F32), beside(corw_ref[3], corw_ref[2], low16)], axis=1)
    own = jnp.concatenate([lev_ref[...].astype(F32), beside(colw_ref[1], colw_ref[0], low)], axis=1)
    depth = jnp.concatenate(
        [jnp.where(inner_south, below, 0.0), own, jnp.where(inner_north, above, 0.0)], axis=0
    ) / NLEV
    hu = 0.5 * (depth + pltpu.roll(depth, 1, 1))
    hv = 0.5 * (depth + pltpu.roll(depth, 1, 0))
    for ref, value in (
        (hu_ref, hu), (hue_ref, pltpu.roll(hu, width - 1, 1)),
        (hv_ref, hv), (hvu_ref, pltpu.roll(hv, rows + 31, 0)),
    ):
        ref[...] = value[8 : height + 8]

    sub = iota((8, width), 0)
    first, last = sub == 0, sub == 7
    keep_south = jnp.where(inner_south, 1.0, 0.0)
    keep_north = jnp.where(inner_north, 1.0, 0.0)
    n_tiles = height // 8

    def advance(m, before):
        n_cur = state[m, NORTH, 0:8, :]
        n_roll = pltpu.roll(n_cur, 7, 0)
        g_before = es_before = None
        held = []
        for k in range(n_tiles):
            at = slice(8 * k, 8 * k + 8)
            e = state[m, EAST, at, :]
            n = n_cur
            row = (lat * rows + (8 * k - 8) + iota((8, LANES), 0)).astype(F32)
            cu = 0.25 * (CORI_BASE + CORI_SLOPE * (row + 0.5) / total_rows)
            cv = 0.25 * (CORI_BASE + CORI_SLOPE * row / total_rows)
            cu = jnp.concatenate([cu] * (width // LANES), axis=1)
            cv = jnp.concatenate([cv] * (width // LANES), axis=1)
            if k + 1 < n_tiles:
                n_cur = state[m, NORTH, 8 * k + 8 : 8 * k + 16, :]
                n_next = pltpu.roll(n_cur, 7, 0)
                n_up = jnp.where(last, n_next, n_roll)
                n_roll = n_next
            else:
                n_up = n_roll
            e_e = pltpu.roll(e, width - 1, 1)
            new = state[m, LEVEL, at, :] - (
                (hue_ref[at, :] * e_e - hu_ref[at, :] * e) + (hvu_ref[at, :] * n_up - hv_ref[at, :] * n)
            )
            keep = {0: keep_south, n_tiles - 1: keep_north}.get(k)
            if keep is not None:
                new = new * keep
            g = GRAVITY * new
            g_w = pltpu.roll(g, 1, 1)
            g_roll = pltpu.roll(g, 1, 0)
            g_s = g_roll if k == 0 else jnp.where(first, g_before, g_roll)
            g_before = g_roll
            ns = n + n_up
            v_sum = ns + pltpu.roll(ns, 1, 1)
            es = e + e_e
            es_roll = pltpu.roll(es, 1, 0)
            u_sum = es + (es_roll if k == 0 else jnp.where(first, es_before, es_roll))
            es_before = es_roll
            e_new = (1.0 - DRAG_RATE) * e + (cu * v_sum - (g - g_w) + state[m, FORCE, at, :])
            n_new = (1.0 - DRAG_RATE) * n - (cv * u_sum + (g - g_s))
            if keep is not None:
                e_new = e_new * keep
                n_new = n_new * keep
            state[m, LEVEL, at, :] = new
            state[m, EAST, at, :] = e_new
            state[m, NORTH, at, :] = n_new
            if 0 < k < n_tiles - 1:
                held.append(
                    [block_transposed(new[:, c * LANES : (c + 1) * LANES]) for c in range(cols // LANES)]
                )
                if len(held) == 2:
                    for c in range(cols // LANES):
                        i = (k // 2 - 1) * (cols // LANES) + c
                        patches[16 * i : 16 * i + 16, :] = jnp.concatenate(
                            [held[0][c], held[1][c]], axis=0
                        ).astype(BF16)
                    held = []

        item = before + 1
        cells = patches[...]
        act = jnp.tanh(jnp.dot(cells, conv_ref[...], preferred_element_type=F32))
        part[item // GROUP, pl.ds(lax.rem(item, GROUP), 1)] = jnp.sum(act, axis=0, keepdims=True) * inv_root
        high, rest = halves_of(1.0 - act * act)
        gram[item] = lax.dot_general(
            cells, high, ROWS_OVER, preferred_element_type=F32
        ) + lax.dot_general(cells, rest, ROWS_OVER, preferred_element_type=F32)

    def exchange(count, peer, source, target, sends, recvs):
        def copy(d):
            to, device = peer(d)
            return pltpu.make_async_remote_copy(
                src_ref=source(to), dst_ref=target(d), send_sem=sends.at[d],
                recv_sem=recvs.at[d], device_id=device, device_id_type=MESH,
            )

        def start(d, carry):
            copy(d).start()
            return carry

        def finish(d, carry):
            copy(d).wait()
            return carry

        return (
            lambda: lax.fori_loop(1, count, start, 0),
            lambda: lax.fori_loop(1, count, finish, 0),
        )

    def share_parts(h):
        return exchange(
            n_lon, lon_peer, lambda to: part.at[h], lambda d: parts.at[lon, h],
            part_send.at[h], part_recv.at[h],
        )

    shared = ((0, n_items - STEPS), (n_items - STEPS, n_items))

    def share_sums(i):
        at = slice(*shared[i])
        return exchange(
            n_plane, plane_peer, lambda to: all_sum.at[plane, at], lambda d: all_sum.at[plane, at],
            sum_send.at[i], sum_recv.at[i],
        )

    def summarize(h):
        share_parts(h)[1]()
        total = parts[0, h]
        for other in range(1, n_lon):
            total = total + parts[other, h]
        for r in range(GROUP):
            all_sum[plane, pl.ds(h * GROUP + r, 1), :] = total[r : r + 1]

        for i, (_, end) in enumerate(shared):
            @pl.when(h == end // GROUP - 1)
            def _():
                share_sums(i)[0]()

    def stores(m):
        own = (own_rows, own_cols)
        return [
            pltpu.make_async_copy(state.at[(m, LEVEL) + own], sea_out.at[m], store_sem.at[m, 0]),
            pltpu.make_async_copy(state.at[(m, EAST) + own], vel_out.at[0, m], store_sem.at[m, 1]),
            pltpu.make_async_copy(state.at[(m, NORTH) + own], vel_out.at[1, m], store_sem.at[m, 2]),
        ]

    n_groups = n_items // GROUP

    def part_done(h):
        parts[lon, h] = part[h]
        share_parts(h)[0]()

    def some_steps(h, carry):
        m = h // (STEPS // GROUP)

        @pl.when(lax.rem(h, STEPS // GROUP) == 0)
        def _():
            for side in (0, 1):
                row_copy(m, side).wait()

            @pl.when(lat == 0)
            def _():
                state[m, :, 0:8, :] = jnp.zeros((4, 8, width), F32)

            @pl.when(lat == n_lat - 1)
            def _():
                state[m, :, rows + 8 :, :] = jnp.zeros((4, 8, width), F32)

        def one(step, inner):
            item = h * GROUP + step
            advance(m, item - 1)
            return inner

        lax.fori_loop(0, GROUP, one, 0)

        @pl.when(lax.rem(h, STEPS // GROUP) == STEPS // GROUP - 1)
        def _():
            for store in stores(m):
                store.start()
        part_done(h)

        @pl.when(h >= LAG)
        def _():
            summarize(h - LAG)

        return carry

    lax.fori_loop(0, n_groups, some_steps, 0)
    def slopes(first_row, end_row, total):
        at = slice(first_row, end_row)
        _, _, d_hidden = flow_gradients(
            near_par[at], halves_of(all_sum[plane, at, :]), w_low, w_sum, b_in, w_out_pad, b_out
        )
        ds_ref[at] = product(halves_of(d_hidden), w_sum, COLS_OVER) * inv_root
        return lax.fori_loop(
            first_row, end_row, lambda j, acc: acc + gram[j] * ds_ref[pl.ds(j, 1), :], total
        )

    final = n_items - 8
    for h in range(n_groups - LAG, final // GROUP):
        summarize(h)
    conv_grad = slopes(0, final, jnp.zeros(gram.shape[1:], F32))
    for h in range(max(n_groups - LAG, final // GROUP), n_groups):
        summarize(h)
    conv_grad = slopes(final, n_items, conv_grad)
    halves = feat // LANES
    for i in range(PH * PW // 8):
        for h in range(halves):
            near_grad[i * halves + h] = conv_grad[8 * i : 8 * i + 8, h * LANES : (h + 1) * LANES]
    per = near_grad.shape[0] // n_wide
    start, finish = exchange(
        n_wide, wide_peer, lambda to: near_grad.at[pl.ds(to * per, per)], lambda d: got_grad.at[d],
        grad_send.at[0], grad_recv.at[0],
    )
    start()

    for q in range(per_dev):
        item = lon * per_dev + q
        summary_ref[q : q + 1, :] = all_sum[
            plane, pl.ds(lax.rem(item, members) * STEPS + item // members, 1), :
        ]

    for i in range(len(shared)):
        share_sums(i)[1]()
    n_all = iota((n_plane * n_items, n_members), 0)
    all_params = params_of(n_all, lax.rem(n_all // n_items, n_grp))
    summ = halves_of(all_sum[...].reshape(n_plane * n_items, feat))
    hidden, d_raw, d_hidden = flow_gradients(all_params, summ, w_low, w_sum, b_in, w_out_pad, b_out)

    got_grad[0] = near_grad[pl.ds(wide * per, per)]
    finish()
    total = got_grad[0]
    for d in range(1, n_wide):
        total = total + got_grad[d]
    mid_grad[z] = total
    start, finish = exchange(
        n_z, z_peer, lambda to: mid_grad.at[z], lambda d: mid_grad.at[z], grad_send.at[1], grad_recv.at[1]
    )
    start()

    conv_rows = PH * PW * feat // LANES
    w_cols = hid // LANES
    flat_ref[...] = jnp.zeros_like(flat_ref)
    d_halves = halves_of(d_hidden)
    g_low = product(halves_of(all_params), d_halves, ROWS_OVER)[:HALF]
    g_sum = product(summ, d_halves, ROWS_OVER)
    for h in range(w_cols):
        flat_ref[pl.ds(conv_rows + h, HALF, stride=w_cols), :] = g_low[:, h * LANES : (h + 1) * LANES]
        flat_ref[pl.ds(conv_rows + HALF * w_cols + h, feat, stride=w_cols), :] = g_sum[
            :, h * LANES : (h + 1) * LANES
        ]

    finish()
    total = mid_grad[0]
    for d in range(1, n_z):
        total = total + mid_grad[d]
    mine = pl.ds(wide * per, per)
    end_grad[mine] = total
    start, finish = exchange(
        n_wide, wide_peer, lambda to: end_grad.at[mine], lambda d: end_grad.at[mine],
        grad_send.at[2], grad_recv.at[2],
    )
    start()

    base = conv_rows + (HALF + feat) * w_cols
    g_b_in = jnp.sum(d_hidden, axis=0, keepdims=True)
    for h in range(w_cols):
        flat_ref[base + h : base + h + 1, :] = g_b_in[:, h * LANES : (h + 1) * LANES]
    base += w_cols
    out_pad[...] = product(halves_of(hidden), halves_of(d_raw), ROWS_OVER)
    per_row = LANES // (2 * HALF)
    out_rows = hid // per_row
    packed = out_pad[pl.ds(0, out_rows, stride=per_row), :]
    for s in range(1, per_row):
        packed = packed + pltpu.roll(
            out_pad[pl.ds(s, out_rows, stride=per_row), :], s * 2 * HALF, 1
        )
    flat_ref[base : base + out_rows, :] = packed
    base += out_rows
    flat_ref[base : base + 1, :] = jnp.sum(d_raw, axis=0, keepdims=True)
    for m in range(members):
        for store in stores(m):
            store.wait()

    finish()
    for i in range(PH * PW // 8):
        for h in range(halves):
            flat_ref[pl.ds(8 * i * halves + h, 8, stride=halves), :] = end_grad[i * halves + h]


def finish_kernel(
    flat_size, flat_ref, summary_ref, sea_ref, vel_ref, flat_out, summary_out, sea_out, vel_out,
    flat, summary, held, load_sem, store_sem,
):
    members = sea_ref.shape[0]
    moves = [(flat_ref, flat, flat_out), (summary_ref, summary, summary_out)]
    moves += [(sea_ref.at[m], held.at[m], sea_out.at[m]) for m in range(members)]
    moves += [
        (vel_ref.at[i, m], held.at[members * (i + 1) + m], vel_out.at[i, m])
        for i in (0, 1) for m in range(members)
    ]
    loads = [pltpu.make_async_copy(a, b, load_sem.at[i]) for i, (a, b, _) in enumerate(moves)]
    stores = [pltpu.make_async_copy(b, c, store_sem.at[i]) for i, (_, b, c) in enumerate(moves)]
    for load in loads:
        load.start()
    loads[0].wait()
    total = flat[...]
    mean = jnp.sum(jnp.sum(total * total, axis=0, keepdims=True), axis=1, keepdims=True) / flat_size
    flat[...] = total * (-1.0 / jnp.sqrt(mean + EPSILON))
    stores[0].start()
    for load, store in zip(loads[1:], stores[1:]):
        load.wait()
        store.start()
    for store in stores:
        store.wait()


def shards(
    sea_surface, velocity, levels, wind_basis, proposals, member_ids, conv_weight,
    couple_in, couple_in_bias, couple_out, couple_out_bias,
):
    members, rows, cols = sea_surface.shape
    n_lon, n_lat, n_grp = lax.axis_size("lon"), lax.axis_size("lat"), lax.axis_size("grp")
    n_z = n_lon // 2
    n_plane = n_lat * n_grp
    n_wide = n_lon // n_z * n_plane
    n_items = members * STEPS
    per_dev = n_items // n_lon
    cells, feat = conv_weight.shape
    hid = couple_in.shape[1]
    height, width = rows + 16, cols + LANES
    weights = (couple_in, couple_in_bias, couple_out, couple_out_bias)
    flat_size = cells * feat + sum(w.size for w in weights)
    flat_rows = -(-flat_size // (8 * LANES)) * 8
    pieces = cells // 8 * (feat // LANES)
    per = pieces // n_wide
    shape = jax.ShapeDtypeStruct
    vmem, dma = pltpu.VMEM, pltpu.SemaphoreType.DMA
    summary, flat, sea, vel = pl.pallas_call(
        functools.partial(main_kernel, n_z),
        out_shape=(
            shape((per_dev, feat), F32),
            shape((flat_rows, LANES), F32),
            shape(sea_surface.shape, F32),
            shape(velocity.shape, F32),
        ),
        in_specs=[SMEM] * 2 + [VMEM] * 7 + [ANY] * 4,
        out_specs=(VMEM, VMEM, ANY, ANY),
        scratch_shapes=[
            vmem((members, 4, height, width), F32),
            vmem(wind_basis.shape, BF16),
            vmem(couple_in.shape, F32),
            vmem((height, width), F32),
            vmem((height, width), F32),
            vmem((height, width), F32),
            vmem((height, width), F32),
            vmem((rows // PH * (cols // PW), cells), BF16),
            vmem((n_items + 1, cells, feat), F32),
            vmem((rows, LANES), F32),
            vmem((rows, LANES), F32),
            vmem((rows, LANES), F32),
            vmem((rows, LANES), F32),
            vmem((2, 16, cols), jnp.int32),
            vmem((2, rows, LANES), F32),
            vmem((2, rows, LANES), F32),
            vmem((4, 8, LANES), F32),
            vmem((4, 16, LANES), F32),
            vmem((proposals.shape[0], LANES), F32),
            vmem((2, LANES, hid), BF16),
            vmem((2, feat, hid), BF16),
            vmem((2, LANES, hid), BF16),
            vmem((1, LANES), F32),
            vmem((n_items, LANES), F32),
            vmem((n_items // GROUP + 1, GROUP, feat), F32),
            vmem((n_lon, n_items // GROUP, GROUP, feat), F32),
            vmem((n_plane, n_items, feat), F32),
            vmem((n_items, feat), F32),
            vmem((pieces, 8, LANES), F32),
            vmem((n_wide, per, 8, LANES), F32),
            vmem((n_z, per, 8, LANES), F32),
            vmem((pieces, 8, LANES), F32),
            vmem((hid, LANES), F32),
            dma((5,)),
            dma((members, 3)),
            dma((members, 2)),
            dma((members, 2)),
            dma((16,)),
            dma((16,)),
            dma((n_items // GROUP, n_lon)),
            dma((n_items // GROUP, n_lon)),
            dma((2, n_plane)),
            dma((2, n_plane)),
            dma((3, n_wide)),
            dma((3, n_wide)),
        ],
        compiler_params=pltpu.CompilerParams(collective_id=0, has_side_effects=True),
        name="ensemble",
    )(
        member_ids, proposals, member_ids.reshape(1, -1), proposals, levels, conv_weight,
        couple_in_bias.reshape(1, -1), couple_out.T, couple_out_bias.reshape(1, -1),
        sea_surface, velocity, wind_basis, couple_in,
    )
    flat, summary, sea, vel = pl.pallas_call(
        functools.partial(finish_kernel, float(flat_size)),
        out_shape=(
            shape(flat.shape, F32), shape(summary.shape, F32), shape(sea.shape, F32), shape(vel.shape, F32),
        ),
        in_specs=[ANY] * 4,
        out_specs=(ANY,) * 4,
        scratch_shapes=[
            vmem(flat.shape, F32),
            vmem(summary.shape, F32),
            vmem((3 * members, rows, cols), F32),
            dma((3 * members + 2,)),
            dma((3 * members + 2,)),
        ],
        name="finish",
    )(flat, summary, sea, vel)
    return sea, vel, summary.reshape((1, 1, 1) + summary.shape), flat.reshape(-1)[:flat_size]


def solution(mesh):
    in_specs = (
        P("grp", "lat", "lon"),
        P(None, "grp", "lat", "lon"),
        P("lat", "lon"),
        P(None, "lat", "lon"),
        P(), P(), P(), P(), P(), P(), P(),
    )
    out_specs = (
        P("grp", "lat", "lon"),
        P(None, "grp", "lat", "lon"),
        P("lon", "lat", "grp", None, None),
        P(),
    )
    return jax.shard_map(shards, mesh=mesh, in_specs=in_specs, out_specs=out_specs, check_vma=False)
```
